1024 devices in a mesh: region: 8 (over y_hi, x), dom: 128 (over y_lo, z, core).
Axes of the slice: x: 4, y: 4 (y_hi: 2, y_lo: 2; y = y_hi * 2 + y_lo), z: 32, core: 2. Of those that a mesh axis runs over, the one named last changes fastest.
Arguments:
- displacement: float32 [3, 1048576], P(None, ('region', 'dom')), may hold values from -6 to 6
- velocity: float32 [3, 1048576], P(None, ('region', 'dom')), may hold values from -6 to 6
- acceleration: float32 [3, 1048576], P(None, ('region', 'dom')), may hold values from -6 to 6
- solid_mass_inverse: float32 [1048576], P(('region', 'dom')), may hold values from 0.05 to 0.3
- connectivity: int32 [125, 32768], P(None, ('region', 'dom')), may hold values from 0 to 1023
- lame_lambda: bfloat16 [125, 32768], P(None, ('region', 'dom')), may hold values from 0.5 to 2
- shear_modulus: bfloat16 [125, 32768], P(None, ('region', 'dom')), may hold values from 0.29882812 to 1.5
- inverse_size: float32 [32768], P(('region', 'dom')), may hold values from 0.7 to 1.4
- potential: float32 [524288], P(('region', 'dom')), may hold values from -6 to 6
- potential_dot: float32 [524288], P(('region', 'dom')), may hold values from -6 to 6
- potential_ddot: float32 [524288], P(('region', 'dom')), may hold values from -6 to 6
- fluid_mass_inverse: float32 [524288], P(('region', 'dom')), may hold values from 0.1 to 0.5
- fluid_connectivity: int32 [125, 16384], P(None, ('region', 'dom')), may hold values from 0 to 511
- density_inverse: bfloat16 [125, 16384], P(None, ('region', 'dom')), may hold values from 0.5 to 2
- fluid_inverse_size: float32 [16384], P(('region', 'dom')), may hold values from 0.7 to 1.4
- solid_halo: int32 [2, 98304], P(None, ('region', 'dom')), may hold values from 0 to 1023, as said below
- fluid_halo: int32 [2, 49152], P(None, ('region', 'dom')), may hold values from 0 to 511, as said below
- solid_interface: int32 [2, 1048576], P(None, ('region', 'dom')), may hold values from -1 to 1023, as said below
- fluid_interface: int32 [2, 1048576], P(None, ('region', 'dom')), may hold values from -1 to 511, as said below
- interface_normal: float32 [3, 2, 1048576], P(None, None, ('region', 'dom')), may hold values from -6 to 6
Outputs:
- velocity_new: float32 [3, 1048576], P(None, ('region', 'dom'))
- acceleration_new: float32 [3, 1048576], P(None, ('region', 'dom'))
- potential_dot_new: float32 [524288], P(('region', 'dom'))
- potential_ddot_new: float32 [524288], P(('region', 'dom'))
The draws below stay inside these ranges and needn't reach their ends.
Inputs may be any that keep to these rules, and one draw needn't show every extreme that they name: `solid_halo`: on each partition the 96 nodes of row 0 and of row 1 are all different. Column k of row 1 on dom index d and column k of row 0 on dom index d + 1 (cyclically, same region index) name one node shared by the two partitions. `fluid_halo`: on each partition the 48 nodes of row 0 and of row 1 are all different. Column k of row 1 on dom index d and column k of row 0 on dom index d + 1 (cyclically, same region index) name one node shared by the two partitions. -1 marks an empty slot, and the live slots of each row come first. Slot k of row 1 on partition (r, d) pairs with slot k of row 0 of fluid_interface on partition (r + 1, d), and slot k of row 0 on (r, d) with slot k of row 1 of fluid_interface on (r - 1, d); both are live or both empty. Row 0 of region index 0 and row 1 of region index 7 are empty; every other row holds more than half of 1024 live slots. For every region index r below 7 and every dom index, row 1 of solid_interface on (r, d) or row 1 of fluid_interface on (r, d) is full (1024 live slots). A node may stand in several slots. `fluid_interface`: -1 marks an empty slot, and the live slots of each row come first; pairing as stated for solid_interface. Row 0 of region index 0 and row 1 of region index 7 are empty; every other row holds more than half of 1024 live slots.
All inputs are finite; a program needn't handle non-finite values.
Results may differ from the reference program's by a relative error of at most 0.0003.
Values sent between devices are 32-bit elements; how exact they have to be, the bound alone decides.
A program may use at most 32 MiB of HBM per device.

```python
import math
import jax
import jax.numpy as jnp
import numpy as np
from jax import lax

ELEM = 32
IFACE = 1024
FELEM = 16
NODES = 1024
FNODES = 512
HALO = 96
FHALO = 48
N_REGION = 8
N_DOM = 128


def distinct_rims(key, node_total, rim_size):
    device_total = N_REGION * N_DOM
    device_keys = jax.random.split(key, device_total)
    chosen = lax.map(lambda device_key: jax.random.permutation(device_key, node_total)[:2 * rim_size].astype(jnp.int32), device_keys)
    return chosen.reshape(device_total, 2, rim_size).transpose(1, 0, 2).reshape(2, device_total * rim_size)


def draw_solid_halo(key, part):
    return distinct_rims(jax.random.fold_in(key, 3), NODES, HALO)


def draw_fluid_halo(key, part):
    return distinct_rims(jax.random.fold_in(key, 4), FNODES, FHALO)


def boundary_counts(key):
    count_key = jax.random.fold_in(key, 11)
    key_count, key_full = jax.random.split(count_key, 2)
    counts = jax.random.randint(key_count, (N_REGION - 1, N_DOM, 2), IFACE // 2 + 1, IFACE + 1)
    position = jax.random.randint(key_full, (N_REGION - 1, N_DOM, 1), 0, 2)
    columns = lax.broadcasted_iota(jnp.int32, (N_REGION - 1, N_DOM, 2), 2)
    return jnp.where(columns == position, IFACE, counts).astype(jnp.int32)


def interface_slots(key, live_counts, node_total, salt_value):
    value_key = jax.random.fold_in(key, salt_value)
    values = jax.random.randint(value_key, (2, N_REGION, N_DOM, IFACE), 0, node_total)
    slot_ids = lax.broadcasted_iota(jnp.int32, values.shape, 3)
    chosen = jnp.where(slot_ids < live_counts[..., None], values, -1)
    return chosen.reshape(2, N_REGION * N_DOM * IFACE).astype(jnp.int32)


def live_rows(counts, upper_direction, lower_direction):
    empty = jnp.zeros((1, N_DOM), jnp.int32)
    lower_row = jnp.concatenate([empty, counts[:, :, lower_direction]], axis=0)
    upper_row = jnp.concatenate([counts[:, :, upper_direction], empty], axis=0)
    return jnp.stack([lower_row, upper_row], axis=0).astype(jnp.int32)


def draw_solid_interface(key, part):
    counts = boundary_counts(key)
    return interface_slots(key, live_rows(counts, 0, 1), NODES, 21)


def draw_fluid_interface(key, part):
    counts = boundary_counts(key)
    return interface_slots(key, live_rows(counts, 1, 0), FNODES, 22)


def place_ends(result, key, smallest, top_value):
    shape = result.shape
    place = [jax.random.randint(jax.random.fold_in(key, axis), (), 0, shape[axis]) for axis in range(len(shape))]
    result = result.at[tuple(place)].set(smallest)
    longest = shape.index(max(shape))
    place[longest] = (place[longest] + 1) % shape[longest]
    return result.at[tuple(place)].set(top_value)


def shard_levels(stream_key, shape, cuts, smallest, high):
    gain = 1.0
    for axis_at, parts in cuts:
        steps = jax.random.uniform(jax.random.fold_in(jax.random.fold_in(stream_key, 6), axis_at), (parts,), jnp.float32, smallest / len(cuts), high / len(cuts))
        gain = gain * jnp.repeat(jnp.exp(steps), shape[axis_at] // parts).reshape((-1,) + (1,) * (len(shape) - 1 - axis_at))
    return gain


def normal_values(key, shape, width, bound, shards=(), held_as=jnp.bfloat16):
    values = width * jax.random.normal(key, shape, jnp.float32)
    if shards:
        values = values * shard_levels(key, shape, shards, -0.22, 0.18)
    return jnp.clip(values, -bound, bound).astype(held_as)


def setup_inputs(seed: int = 0) -> dict:
    seeds = jax.random.split(jax.random.key(seed), 21)
    displacement = normal_values(seeds[0], (3, NODES * N_REGION * N_DOM), 1.0, 6.0, ((1, 1024),), jnp.float32)
    velocity = normal_values(seeds[1], (3, NODES * N_REGION * N_DOM), 1.0, 6.0, ((1, 1024),), jnp.float32)
    acceleration = normal_values(seeds[2], (3, NODES * N_REGION * N_DOM), 1.0, 6.0, ((1, 1024),), jnp.float32)
    solid_mass_inverse = jnp.clip(jnp.exp(math.log(0.3) - 1.7917595 * jax.random.uniform(seeds[3], (NODES * N_REGION * N_DOM,), jnp.float32) ** shard_levels(seeds[3], (NODES * N_REGION * N_DOM,), ((0, 1024),), -0.2, 0.2)), 0.05, 0.3)
    connectivity = place_ends(jax.random.randint(seeds[4], (125, ELEM * N_REGION * N_DOM), 0, NODES), jax.random.fold_in(seeds[4], 1), 0, NODES - 1).astype(jnp.int32)
    lame_lambda = jnp.clip(jnp.exp(math.log(2.0) - 1.3862944 * jax.random.uniform(seeds[5], (125, ELEM * N_REGION * N_DOM), jnp.float32) ** shard_levels(seeds[5], (125, ELEM * N_REGION * N_DOM), ((1, 1024),), -0.2, 0.2)), 0.5, 2.0).astype(jnp.bfloat16)
    shear_modulus = jnp.clip(jnp.exp(math.log(1.5) - 1.6133518 * jax.random.uniform(seeds[6], (125, ELEM * N_REGION * N_DOM), jnp.float32) ** shard_levels(seeds[6], (125, ELEM * N_REGION * N_DOM), ((1, 1024),), -0.2, 0.2)), 0.29882812, 1.5).astype(jnp.bfloat16)
    inverse_size = jnp.clip(jnp.exp(math.log(1.4) - 0.6931472 * jax.random.uniform(seeds[7], (ELEM * N_REGION * N_DOM,), jnp.float32) ** shard_levels(seeds[7], (ELEM * N_REGION * N_DOM,), ((0, 1024),), -0.2, 0.2)), 0.7, 1.4)
    potential = normal_values(seeds[8], (FNODES * N_REGION * N_DOM,), 1.0, 6.0, ((0, 1024),), jnp.float32)
    potential_dot = normal_values(seeds[9], (FNODES * N_REGION * N_DOM,), 1.0, 6.0, ((0, 1024),), jnp.float32)
    potential_ddot = normal_values(seeds[10], (FNODES * N_REGION * N_DOM,), 1.0, 6.0, ((0, 1024),), jnp.float32)
    fluid_mass_inverse = jnp.clip(jnp.exp(math.log(0.5) - 1.609438 * jax.random.uniform(seeds[11], (FNODES * N_REGION * N_DOM,), jnp.float32) ** shard_levels(seeds[11], (FNODES * N_REGION * N_DOM,), ((0, 1024),), -0.2, 0.2)), 0.1, 0.5)
    fluid_connectivity = place_ends(jax.random.randint(seeds[12], (125, FELEM * N_REGION * N_DOM), 0, FNODES), jax.random.fold_in(seeds[12], 1), 0, FNODES - 1).astype(jnp.int32)
    density_inverse = jnp.clip(jnp.exp(math.log(2.0) - 1.3862944 * jax.random.uniform(seeds[13], (125, FELEM * N_REGION * N_DOM), jnp.float32) ** shard_levels(seeds[13], (125, FELEM * N_REGION * N_DOM), ((1, 1024),), -0.2, 0.2)), 0.5, 2.0).astype(jnp.bfloat16)
    fluid_inverse_size = jnp.clip(jnp.exp(math.log(1.4) - 0.6931472 * jax.random.uniform(seeds[14], (FELEM * N_REGION * N_DOM,), jnp.float32) ** shard_levels(seeds[14], (FELEM * N_REGION * N_DOM,), ((0, 1024),), -0.2, 0.2)), 0.7, 1.4)
    solid_halo = draw_solid_halo(jax.random.fold_in(seeds[20], 71), 0)
    fluid_halo = draw_fluid_halo(jax.random.fold_in(seeds[20], 71), 0)
    solid_interface = draw_solid_interface(jax.random.fold_in(seeds[20], 71), 0)
    fluid_interface = draw_fluid_interface(jax.random.fold_in(seeds[20], 71), 0)
    interface_normal = normal_values(seeds[19], (3, 2, IFACE * N_REGION * N_DOM), 1.0, 6.0, ((2, 1024),), jnp.float32)
    return dict(displacement=displacement, velocity=velocity, acceleration=acceleration, solid_mass_inverse=solid_mass_inverse, connectivity=connectivity, lame_lambda=lame_lambda, shear_modulus=shear_modulus, inverse_size=inverse_size, potential=potential, potential_dot=potential_dot, potential_ddot=potential_ddot, fluid_mass_inverse=fluid_mass_inverse, fluid_connectivity=fluid_connectivity, density_inverse=density_inverse, fluid_inverse_size=fluid_inverse_size, solid_halo=solid_halo, fluid_halo=fluid_halo, solid_interface=solid_interface, fluid_interface=fluid_interface, interface_normal=interface_normal)


time_step = 0.4

def gll_tables():
    points = np.array([-1.0, -math.sqrt(3.0 / 7.0), 0.0, math.sqrt(3.0 / 7.0), 1.0])
    weights = np.array([0.1, 49.0 / 90.0, 32.0 / 45.0, 49.0 / 90.0, 0.1])
    products = np.array([np.prod([points[row_index] - points[column] for column in range(5) if column != row_index]) for row_index in range(5)])
    derivative = np.zeros((5, 5))
    for row_index in range(5):
        for col_index in range(5):
            if row_index != col_index:
                derivative[row_index, col_index] = products[row_index] / (products[col_index] * (points[row_index] - points[col_index]))
            else:
                derivative[row_index, col_index] = sum((1.0 / (points[row_index] - points[column]) for column in range(5) if column != row_index))
    weight_cube = weights[:, None, None] * weights[None, :, None] * weights[None, None, :]
    return (jnp.asarray(derivative, jnp.float32), jnp.asarray(weight_cube, jnp.float32))

def derivatives_of(derivative, values):
    highest = lax.Precision.HIGHEST
    along_first = jnp.einsum('il,...ljke->...ijke', derivative, values, precision=highest)
    along_second = jnp.einsum('jl,...ilke->...ijke', derivative, values, precision=highest)
    along_third = jnp.einsum('kl,...ijle->...ijke', derivative, values, precision=highest)
    return (along_first, along_second, along_third)

def divergence_of(derivative, along_first, along_second, along_third):
    highest = lax.Precision.HIGHEST
    return jnp.einsum('il,...ijke->...ljke', derivative, along_first, precision=highest) + jnp.einsum('jl,...ijke->...ilke', derivative, along_second, precision=highest) + jnp.einsum('kl,...ijke->...ijle', derivative, along_third, precision=highest)

def solid_element_forces(displaced, connectivity, lame_lambda, shear_modulus, inverse_size, derivative, weight_cube):
    element_count = connectivity.shape[1]
    node_count = displaced.shape[1]
    local_values = displaced[:, connectivity].reshape(3, 5, 5, 5, element_count)
    gradient = jnp.stack(derivatives_of(derivative, local_values), axis=1) * inverse_size
    lame_values = lame_lambda.astype(jnp.float32).reshape(5, 5, 5, element_count)
    shear_values = shear_modulus.astype(jnp.float32).reshape(5, 5, 5, element_count)
    trace_value = gradient[0, 0] + gradient[1, 1] + gradient[2, 2]
    identity = jnp.eye(3, dtype=jnp.float32)[:, :, None, None, None, None]
    stress = lame_values * trace_value * identity + shear_values * (gradient + jnp.swapaxes(gradient, 0, 1))
    weighted = stress * (weight_cube[:, :, :, None] / (inverse_size * inverse_size))
    element_force = -divergence_of(derivative, weighted[:, 0], weighted[:, 1], weighted[:, 2])
    return jnp.zeros((3, node_count), jnp.float32).at[:, connectivity].add(element_force.reshape(3, 125, element_count))

def fluid_element_forces(potential_values, connectivity, density_inverse, inverse_size, derivative, weight_cube):
    element_count = connectivity.shape[1]
    node_count = potential_values.shape[0]
    local_values = potential_values[connectivity].reshape(5, 5, 5, element_count)
    gradient = jnp.stack(derivatives_of(derivative, local_values), axis=0) * inverse_size
    factor = weight_cube[:, :, :, None] * density_inverse.astype(jnp.float32).reshape(5, 5, 5, element_count) / (inverse_size * inverse_size)
    weighted = gradient * factor
    element_force = -divergence_of(derivative, weighted[0], weighted[1], weighted[2])
    return jnp.zeros((node_count,), jnp.float32).at[connectivity].add(element_force.reshape(125, element_count))

def by_part(values, extent):
    part_total = N_REGION * N_DOM
    return jnp.moveaxis(values.reshape(values.shape[:-1] + (part_total, extent)), -2, 0)

def whole(values):
    moved = jnp.moveaxis(values, 0, -2)
    return moved.reshape(moved.shape[:-2] + (moved.shape[-2] * moved.shape[-1],))

def across_regions(values):
    grouped = values.reshape(N_REGION, N_DOM, 2, values.shape[-1])
    empty = jnp.zeros((1, N_DOM, values.shape[-1]), jnp.float32)
    from_lower = jnp.concatenate([empty, grouped[:-1, :, 1]], axis=0)
    from_upper = jnp.concatenate([grouped[1:, :, 0], empty], axis=0)
    return jnp.stack([from_lower, from_upper], axis=2).reshape(N_REGION * N_DOM, 2, values.shape[-1])

def add_slots(totals, indices, contributions):
    target = jnp.where(indices >= 0, indices, totals.shape[-1])
    return totals.at[..., target].add(contributions, mode='drop')

def assemble(totals, rims):
    rim_values = jax.vmap(lambda node_values, rim_index: jnp.moveaxis(node_values[..., rim_index], -2, 0))(totals, rims)
    grouped = rim_values.reshape((N_REGION, N_DOM) + rim_values.shape[1:])
    flat_shape = (N_REGION * N_DOM,) + rim_values.shape[2:]
    from_lower = jnp.roll(grouped[:, :, 1], 1, axis=1).reshape(flat_shape)
    from_upper = jnp.roll(grouped[:, :, 0], -1, axis=1).reshape(flat_shape)

    def add_rims(node_values, rim_index, lower_values, upper_values):
        return node_values.at[..., rim_index[0]].add(lower_values).at[..., rim_index[1]].add(upper_values)
    return jax.vmap(add_rims)(totals, rims, from_lower, from_upper)

def motion_of(values, indices, normals):
    live = indices >= 0
    gathered = values[:, jnp.where(live, indices, 0)]
    return jnp.where(live, lax.optimization_barrier(jnp.sum(normals * gathered, axis=0)), 0.0)

def pressure_of(values, indices):
    live = indices >= 0
    return jnp.where(live, values[jnp.where(live, indices, 0)], 0.0)

def reference(displacement, velocity, acceleration, solid_mass_inverse, connectivity, lame_lambda, shear_modulus, inverse_size, potential, potential_dot, potential_ddot, fluid_mass_inverse, fluid_connectivity, density_inverse, fluid_inverse_size, solid_halo, fluid_halo, solid_interface, fluid_interface, interface_normal):
    derivative, weight_cube = gll_tables()
    half_square = 0.5 * time_step * time_step
    predicted = displacement + time_step * velocity + half_square * acceleration
    fluid_predicted = potential + time_step * potential_dot + half_square * potential_ddot
    solid_parts = by_part(predicted, NODES)
    fluid_parts = by_part(fluid_predicted, FNODES)
    solid_index = by_part(solid_interface, IFACE)
    fluid_index = by_part(fluid_interface, IFACE)
    normal_parts = by_part(interface_normal, IFACE)
    solid_rims = by_part(solid_halo, HALO)
    fluid_rims = by_part(fluid_halo, FHALO)

    def fluid_single(pieces):
        return fluid_element_forces(pieces[0], pieces[1], pieces[2], pieces[3], derivative, weight_cube)
    fluid_force = lax.map(fluid_single, (fluid_parts, by_part(fluid_connectivity, FELEM), by_part(density_inverse, FELEM), by_part(fluid_inverse_size, FELEM)))
    normal_motion = jax.vmap(motion_of)(solid_parts, solid_index, normal_parts)
    arrived_motion = across_regions(normal_motion)
    fluid_force = jax.vmap(add_slots)(fluid_force, fluid_index, arrived_motion)
    fluid_force = assemble(fluid_force, fluid_rims)
    ddot_parts = by_part(fluid_mass_inverse, FNODES) * fluid_force
    potential_ddot_new = whole(ddot_parts)
    potential_dot_new = potential_dot + 0.5 * time_step * (potential_ddot + potential_ddot_new)
    arrived_pressure = across_regions(jax.vmap(pressure_of)(ddot_parts, fluid_index))

    def solid_single(pieces):
        return solid_element_forces(pieces[0], pieces[1], pieces[2], pieces[3], pieces[4], derivative, weight_cube)
    element_force = lax.map(solid_single, (solid_parts, by_part(connectivity, ELEM), by_part(lame_lambda, ELEM), by_part(shear_modulus, ELEM), by_part(inverse_size, ELEM)))
    coupling_force = jax.vmap(add_slots)(jnp.zeros_like(element_force), solid_index, -normal_parts * arrived_pressure[:, None])
    solid_total = assemble(element_force + coupling_force, solid_rims)
    accel_parts = by_part(solid_mass_inverse, NODES)[:, None, :] * solid_total
    acceleration_new = whole(accel_parts)
    velocity_new = velocity + 0.5 * time_step * (acceleration + acceleration_new)
    return (velocity_new, acceleration_new, potential_dot_new, potential_ddot_new)
```

```python
import math

import jax
import jax.numpy as jnp
import numpy as np
from jax import lax
from jax.experimental import pallas as pl
from jax.experimental.pallas import tpu as pltpu
from jax.sharding import PartitionSpec as P

time_step = 0.4
MESH = pl.DeviceIdType.MESH
LANES = 128
f32 = jnp.float32
bf16 = jnp.bfloat16


def gll_tables():
    points = np.array([-1.0, -math.sqrt(3.0 / 7.0), 0.0, math.sqrt(3.0 / 7.0), 1.0])
    weights = np.array([0.1, 49.0 / 90.0, 32.0 / 45.0, 49.0 / 90.0, 0.1])
    products = np.array(
        [np.prod([points[i] - points[j] for j in range(5) if j != i]) for i in range(5)]
    )
    derivative = np.zeros((5, 5))
    for i in range(5):
        for j in range(5):
            if i != j:
                derivative[i, j] = products[i] / (products[j] * (points[i] - points[j]))
            else:
                derivative[i, j] = sum(1.0 / (points[i] - points[k]) for k in range(5) if k != i)
    weight_cube = weights[:, None, None] * weights[None, :, None] * weights[None, None, :]
    return derivative.astype(np.float32), weight_cube.astype(np.float32)


def derivative_matrices():
    derivative, weight_cube = gll_tables()
    eye = np.eye(5, dtype=np.float32)
    whole = np.zeros((3, LANES, LANES), np.float32)
    whole[0, :125, :125] = np.kron(derivative, np.kron(eye, eye))
    whole[1, :125, :125] = np.kron(eye, np.kron(derivative, eye))
    whole[2, :125, :125] = np.kron(eye, np.kron(eye, derivative))
    whole = whole.reshape(3 * LANES, LANES)
    high = whole.astype(jnp.bfloat16)
    low = (whole - high.astype(np.float32)).astype(jnp.bfloat16)
    weights = np.zeros((8, LANES), np.float32)
    weights[:, :125] = weight_cube.reshape(1, 125)
    return high, low, weights


def split(x):
    high = x.astype(bf16)
    return high, (x - high.astype(f32)).astype(bf16)


def dot(a, b, dims):
    return lax.dot_general(a, b, (dims, ((), ())), preferred_element_type=f32)


def dot_split(x, high, low, dims):
    x_high, x_low = split(x)
    return dot(x_high, high, dims) + dot(x_low, high, dims) + dot(x_high, low, dims)


def lookup(tables, hi, lo):
    out = [jnp.zeros(hi.shape, f32) for _ in tables]
    for h in range(len(tables[0])):
        here = hi == h
        for c, rows in enumerate(tables):
            picked = jnp.take_along_axis(
                jnp.broadcast_to(rows[h], hi.shape), lo, axis=1, mode="promise_in_bounds"
            )
            out[c] = jnp.where(here, picked, out[c])
    return out


def mark_low(marks_ref, lo):
    sublane = lax.broadcasted_iota(jnp.int32, (LANES, LANES), 0)
    for row in range(lo.shape[0]):
        line = jnp.broadcast_to(lo[row : row + 1], (LANES, LANES))
        marks_ref[:, row * LANES : (row + 1) * LANES] = jnp.where(line == sublane, 1.0, 0.0).astype(
            bf16
        )


def spread_high(terms_ref, hi, values):
    sublane = lax.broadcasted_iota(jnp.int32, (8, LANES), 0)
    parts = []
    for value in values:
        high = value.astype(bf16).astype(f32)
        parts.append((high, value - high))
    for row in range(hi.shape[0]):
        here = jnp.broadcast_to(hi[row : row + 1], (8, LANES)) == sublane
        for c, pair in enumerate(parts):
            both = [
                jnp.where(here, jnp.broadcast_to(part[row : row + 1], (8, LANES)), 0.0)
                for part in pair
            ]
            terms_ref[16 * c : 16 * c + 16, row * LANES : (row + 1) * LANES] = jnp.concatenate(
                both, axis=0
            ).astype(bf16)


def collect(terms_ref, marks_ref):
    sums = dot(terms_ref[...], marks_ref[...], ((1,), (1,)))
    return [
        sums[16 * c : 16 * c + 8] + sums[16 * c + 8 : 16 * c + 16]
        for c in range(terms_ref.shape[0] // 16)
    ]


def rows_of(ref, lead):
    line = ref[lead]
    return jnp.concatenate([line[:, LANES * t : LANES * (t + 1)] for t in range(8)], axis=0)


def both_sides(ref, *lead):
    return jnp.concatenate(
        [rows_of(ref, (*lead, slice(p, p + 1), slice(None))) for p in range(2)], axis=0
    )


def step_kernel(n_region, n_dom, n_inputs, *refs):
    sources = refs[:n_inputs]
    velocity_out, acceleration_out, dot_out, ddot_out = refs[n_inputs : n_inputs + 4]
    held = refs[n_inputs + 4 : 2 * n_inputs + 4]
    (
        load_sem,
        send_sem,
        recv_sem,
        motion_send,
        motion_recv,
        pressure_send,
        pressure_recv,
        fluid_send,
        fluid_recv,
        solid_send,
        solid_recv,
        index_pad,
        field_pad,
        fluid_index_pad,
        fluid_field_pad,
        element_terms,
        element_marks,
        fluid_terms,
        fluid_marks,
        slot_terms,
        slot_marks,
        arrived_terms,
        arrived_marks,
    ) = refs[2 * n_inputs + 4 :]
    (
        displacement,
        velocity,
        acceleration,
        solid_interface,
        interface_normal,
        potential,
        potential_dot,
        potential_ddot,
        fluid_connectivity,
        density_inverse,
        fluid_inverse_size,
        matrix_high,
        matrix_low,
        weight_cube,
        fluid_interface,
        fluid_halo,
        fluid_mass_inverse,
        connectivity,
        lame_lambda,
        shear_modulus,
        inverse_size,
        solid_halo,
        solid_mass_inverse,
    ) = held

    region, dom = lax.axis_index("region"), lax.axis_index("dom")
    above = (lax.rem(region + 1, n_region), dom)
    below = (lax.rem(region + n_region - 1, n_region), dom)
    upper = (region, lax.rem(dom + 1, n_dom))
    lower = (region, lax.rem(dom + n_dom - 1, n_dom))

    barrier = pltpu.get_barrier_semaphore()
    for other in (above, below, upper, lower):
        pl.semaphore_signal(barrier, inc=1, device_id=other, device_id_type=MESH)
    loads = [
        pltpu.make_async_copy(source, target, load_sem.at[i])
        for i, (source, target) in enumerate(zip(sources, held))
    ]
    for load in loads:
        load.start()

    def send(send_ref, recv_ref, flow, to_higher, to_lower):
        copies = []
        for side, target in ((0, to_higher), (1, to_lower)):
            copy = pltpu.make_async_remote_copy(
                src_ref=send_ref.at[side],
                dst_ref=recv_ref.at[side],
                send_sem=send_sem.at[2 * flow + side],
                recv_sem=recv_sem.at[2 * flow + side],
                device_id=target,
                device_id_type=MESH,
            )
            copy.start()
            copies.append(copy)
        return copies

    for i in range(5):
        loads[i].wait()
    half_square = 0.5 * time_step * time_step
    predicted = displacement[...] + time_step * velocity[...] + half_square * acceleration[...]
    solid_tables = [
        [predicted[c : c + 1, LANES * h : LANES * (h + 1)] for h in range(8)] for c in range(3)
    ]
    slots = both_sides(solid_interface)
    slot_hi, slot_lo = slots >> 7, slots & 127
    normals = [both_sides(interface_normal, c) for c in range(3)]
    moved = lookup(solid_tables, slot_hi, slot_lo)
    motion = normals[0] * moved[0] + normals[1] * moved[1] + normals[2] * moved[2]
    motion_send[0] = motion[8:]
    motion_send[1] = motion[:8]
    pl.semaphore_wait(barrier, 4)
    motion_copies = send(motion_send, motion_recv, 0, above, below)

    for i in range(5, 14):
        loads[i].wait()
    fluid_predicted = (
        potential[...] + time_step * potential_dot[...] + half_square * potential_ddot[...]
    )
    fluid_table = [[fluid_predicted[h : h + 1] for h in range(4)]]
    fluid_index_pad[...] = jnp.full(fluid_index_pad.shape, -1, jnp.int32)
    fluid_index_pad[:, :125] = fluid_connectivity[...]
    fluid_field_pad[...] = jnp.zeros(fluid_field_pad.shape, f32)
    fluid_field_pad[:, :125] = density_inverse[...].astype(f32)
    fluid_index = fluid_index_pad[...]
    fluid_hi, fluid_lo = fluid_index >> 7, fluid_index & 127
    local = lookup(fluid_table, fluid_hi, fluid_lo)[0]
    high, low = matrix_high[...], matrix_low[...]
    gradient = dot_split(local, high, low, ((1,), (1,)))

    def column(line, count):
        rows = lax.broadcasted_iota(jnp.int32, (count, count), 0)
        columns = lax.broadcasted_iota(jnp.int32, (count, count), 1)
        wide = jnp.broadcast_to(line, (count, count))
        return jnp.sum(jnp.where(rows == columns, wide, 0.0), axis=1, keepdims=True)

    weights = weight_cube[0:1]
    fluid_factor = weights * fluid_field_pad[...] * (-1.0 / column(fluid_inverse_size[...], 16))
    weighted = jnp.concatenate(
        [gradient[:, LANES * b : LANES * (b + 1)] * fluid_factor for b in range(3)], axis=1
    )
    element = dot_split(weighted, high, low, ((1,), (0,)))
    mark_low(fluid_marks, fluid_lo)
    spread_high(fluid_terms, fluid_hi, [element])
    fluid_force = collect(fluid_terms, fluid_marks)[0]

    for i in range(14, 17):
        loads[i].wait()
    fluid_slots = both_sides(fluid_interface)
    arrived_hi, arrived_lo = fluid_slots >> 7, fluid_slots & 127
    mark_low(arrived_marks, arrived_lo)
    rim = fluid_halo[...]
    rim_hi, rim_lo = rim >> 7, rim & 127
    lane8 = lax.broadcasted_iota(jnp.int32, (8, LANES), 0) * LANES + lax.broadcasted_iota(
        jnp.int32, (8, LANES), 1
    )
    for copy in motion_copies:
        copy.wait_recv()
    spread_high(
        arrived_terms, arrived_hi, [jnp.concatenate([motion_recv[0], motion_recv[1]], axis=0)]
    )
    fluid_total = fluid_force + collect(arrived_terms, arrived_marks)[0]

    def halo_tables(halo_ref, count):
        found = []
        nodes = halo_ref[...]
        for side in range(2):
            found.append(nodes[side : side + 1])
        return found

    def rim_index(halo_ref, pad_ref, count):
        pad_ref[...] = jnp.full(pad_ref.shape, -1, jnp.int32)
        pad_ref[0:2, :count] = halo_ref[...]
        return pad_ref[...]

    fluid_rim = rim_index(fluid_halo, index_pad.at[0:8], 48)
    rim_values = lookup(
        [[fluid_total[h : h + 1] for h in range(4)]], fluid_rim >> 7, fluid_rim & 127
    )[0]
    fluid_send[0] = rim_values[1:2]
    fluid_send[1] = rim_values[0:1]
    fluid_copies = send(fluid_send, fluid_recv, 1, upper, lower)

    def slot_of_node(rim):
        out = []
        marks_lane = lax.broadcasted_iota(jnp.int32, (LANES, LANES), 0)
        sublane = lax.broadcasted_iota(jnp.int32, (8, LANES), 0)
        number = lax.broadcasted_iota(jnp.int32, (8, LANES), 1).astype(f32) + 1.0
        for side in range(2):
            line = rim[side : side + 1]
            marks = jnp.where(
                jnp.broadcast_to(line & 127, (LANES, LANES)) == marks_lane, 1.0, 0.0
            ).astype(bf16)
            terms = jnp.where(jnp.broadcast_to(line >> 7, (8, LANES)) == sublane, number, 0.0)
            out.append(dot(terms.astype(bf16), marks, ((1,), (1,))).astype(jnp.int32) - 1)
        return out

    def add_rims(total, arrived, places):
        for line, place in zip(arrived, places):
            picked = jnp.take_along_axis(
                jnp.broadcast_to(line, place.shape),
                jnp.maximum(place, 0),
                axis=1,
                mode="promise_in_bounds",
            )
            total = total + jnp.where(place >= 0, picked, 0.0)
        return total

    fluid_places = slot_of_node(fluid_rim)

    for i in range(17, 23):
        loads[i].wait()
    index_pad[...] = jnp.full(index_pad.shape, -1, jnp.int32)
    index_pad[:, :125] = connectivity[...]
    index = index_pad[...]
    hi, lo = index >> 7, index & 127
    values = lookup(solid_tables, hi, lo)
    gradient = dot_split(jnp.concatenate(values, axis=0), high, low, ((1,), (1,)))
    field_pad[...] = jnp.zeros(field_pad.shape, f32)
    field_pad[:, :125] = lame_lambda[...].astype(f32)
    lame = field_pad[...]
    field_pad[:, :125] = shear_modulus[...].astype(f32)
    shear = field_pad[...]
    factor = weights * (-1.0 / column(inverse_size[...], 32))
    lame, shear = lame * factor, shear * factor
    grad = [
        [gradient[32 * c : 32 * c + 32, LANES * b : LANES * (b + 1)] for b in range(3)]
        for c in range(3)
    ]
    trace = lame * (grad[0][0] + grad[1][1] + grad[2][2])
    stress = [[None] * 3 for _ in range(3)]
    for a in range(3):
        stress[a][a] = trace + shear * (grad[a][a] + grad[a][a])
        for b in range(a):
            stress[a][b] = stress[b][a] = shear * (grad[a][b] + grad[b][a])
    weighted = jnp.concatenate([jnp.concatenate(row, axis=1) for row in stress], axis=0)
    element = dot_split(weighted, high, low, ((1,), (0,)))
    mark_low(element_marks, lo)
    spread_high(element_terms, hi, [element[32 * c : 32 * c + 32] for c in range(3)])

    for copy in fluid_copies:
        copy.wait_recv()
    assembled = add_rims(fluid_total, [fluid_recv[0], fluid_recv[1]], fluid_places)
    ddot = fluid_mass_inverse[...] * assembled[:4]
    pressure = lookup([[ddot[h : h + 1] for h in range(4)]], arrived_hi, arrived_lo)[0]
    pressure_send[0] = pressure[8:]
    pressure_send[1] = pressure[:8]
    pressure_copies = send(pressure_send, pressure_recv, 2, above, below)
    ddot_out[...] = ddot
    dot_out[...] = potential_dot[...] + 0.5 * time_step * (potential_ddot[...] + ddot)

    force = collect(element_terms, element_marks)
    mark_low(slot_marks, slot_lo)
    solid_rim = rim_index(solid_halo, index_pad.at[0:8], 96)
    solid_places = slot_of_node(solid_rim)
    for copy in pressure_copies:
        copy.wait_recv()
    arrived = jnp.concatenate([pressure_recv[0], pressure_recv[1]], axis=0)
    spread_high(slot_terms, slot_hi, [-(normal * arrived) for normal in normals])
    coupling = collect(slot_terms, slot_marks)
    total = [a + b for a, b in zip(force, coupling)]
    rim_values = lookup(
        [[t[h : h + 1] for h in range(8)] for t in total], solid_rim >> 7, solid_rim & 127
    )
    for c in range(3):
        solid_send[0, c : c + 1] = rim_values[c][1:2]
        solid_send[1, c : c + 1] = rim_values[c][0:1]
    solid_copies = send(solid_send, solid_recv, 3, upper, lower)
    mass = solid_mass_inverse[...]
    base = [
        rows_of(velocity, (slice(c, c + 1), slice(None)))
        + 0.5 * time_step * rows_of(acceleration, (slice(c, c + 1), slice(None)))
        for c in range(3)
    ]
    for copy in solid_copies:
        copy.wait_recv()
    for c in range(3):
        arrived = [solid_recv[side, c : c + 1] for side in range(2)]
        new = mass * add_rims(total[c], arrived, solid_places)
        speed = base[c] + 0.5 * time_step * new
        for h in range(8):
            acceleration_out[c : c + 1, LANES * h : LANES * (h + 1)] = new[h : h + 1]
            velocity_out[c : c + 1, LANES * h : LANES * (h + 1)] = speed[h : h + 1]
    for copy in motion_copies + fluid_copies + pressure_copies + solid_copies:
        copy.wait_send()


def on_device(
    n_region,
    n_dom,
    displacement,
    velocity,
    acceleration,
    solid_mass_inverse,
    connectivity,
    lame_lambda,
    shear_modulus,
    inverse_size,
    potential,
    potential_dot,
    potential_ddot,
    fluid_mass_inverse,
    fluid_connectivity,
    density_inverse,
    fluid_inverse_size,
    solid_halo,
    fluid_halo,
    solid_interface,
    fluid_interface,
    interface_normal,
):
    high, low, weights = derivative_matrices()
    operands = (
        displacement,
        velocity,
        acceleration,
        solid_interface,
        interface_normal,
        potential.reshape(4, LANES),
        potential_dot.reshape(4, LANES),
        potential_ddot.reshape(4, LANES),
        fluid_connectivity.T,
        density_inverse.T,
        fluid_inverse_size.reshape(1, 16),
        jnp.asarray(high),
        jnp.asarray(low),
        jnp.asarray(weights),
        fluid_interface,
        fluid_halo,
        fluid_mass_inverse.reshape(4, LANES),
        connectivity.T,
        lame_lambda.T,
        shear_modulus.T,
        inverse_size.reshape(1, 32),
        solid_halo,
        solid_mass_inverse.reshape(8, LANES),
    )
    count = len(operands)
    vmem = pltpu.VMEM
    outs = pl.pallas_call(
        lambda *refs: step_kernel(n_region, n_dom, count, *refs),
        out_shape=(
            jax.ShapeDtypeStruct((3, 1024), f32),
            jax.ShapeDtypeStruct((3, 1024), f32),
            jax.ShapeDtypeStruct((4, LANES), f32),
            jax.ShapeDtypeStruct((4, LANES), f32),
        ),
        in_specs=[pl.BlockSpec(memory_space=pl.ANY)] * count,
        out_specs=[pl.BlockSpec(memory_space=vmem)] * 4,
        scratch_shapes=[vmem(x.shape, x.dtype) for x in operands]
        + [
            pltpu.SemaphoreType.DMA((count,)),
            pltpu.SemaphoreType.DMA((8,)),
            pltpu.SemaphoreType.DMA((8,)),
            vmem((2, 8, LANES), f32),
            vmem((2, 8, LANES), f32),
            vmem((2, 8, LANES), f32),
            vmem((2, 8, LANES), f32),
            vmem((2, 1, LANES), f32),
            vmem((2, 1, LANES), f32),
            vmem((2, 3, LANES), f32),
            vmem((2, 3, LANES), f32),
            vmem((32, LANES), jnp.int32),
            vmem((32, LANES), f32),
            vmem((16, LANES), jnp.int32),
            vmem((16, LANES), f32),
            vmem((48, 32 * LANES), bf16),
            vmem((LANES, 32 * LANES), bf16),
            vmem((16, 16 * LANES), bf16),
            vmem((LANES, 16 * LANES), bf16),
            vmem((48, 16 * LANES), bf16),
            vmem((LANES, 16 * LANES), bf16),
            vmem((16, 16 * LANES), bf16),
            vmem((LANES, 16 * LANES), bf16),
        ],
        compiler_params=pltpu.CompilerParams(collective_id=0, has_side_effects=True),
        name="newmark_step",
    )(*operands)
    return outs[0], outs[1], outs[2].reshape(512), outs[3].reshape(512)


def solution(mesh):
    cut = ("region", "dom")
    line, plane = P(cut), P(None, cut)
    in_specs = (
        (plane,) * 3
        + (line,)
        + (plane,) * 3
        + (line,) * 5
        + (plane,) * 2
        + (line,)
        + (plane,) * 4
        + (P(None, None, cut),)
    )
    n_region, n_dom = mesh.shape["region"], mesh.shape["dom"]
    return jax.shard_map(
        lambda *args: on_device(n_region, n_dom, *args),
        mesh=mesh,
        in_specs=in_specs,
        out_specs=(plane, plane, line, line),
        check_vma=False,
    )
```

```python
import math

import jax
import jax.numpy as jnp
import numpy as np
from jax import lax
from jax.experimental import pallas as pl
from jax.experimental.pallas import tpu as pltpu
from jax.sharding import PartitionSpec as P

time_step = 0.4
MESH = pl.DeviceIdType.MESH
LANES = 128
f32 = jnp.float32
bf16 = jnp.bfloat16


def gll_tables():
    points = np.array([-1.0, -math.sqrt(3.0 / 7.0), 0.0, math.sqrt(3.0 / 7.0), 1.0])
    weights = np.array([0.1, 49.0 / 90.0, 32.0 / 45.0, 49.0 / 90.0, 0.1])
    products = np.array(
        [np.prod([points[i] - points[j] for j in range(5) if j != i]) for i in range(5)]
    )
    derivative = np.zeros((5, 5))
    for i in range(5):
        for j in range(5):
            if i != j:
                derivative[i, j] = products[i] / (products[j] * (points[i] - points[j]))
            else:
                derivative[i, j] = sum(1.0 / (points[i] - points[k]) for k in range(5) if k != i)
    weight_cube = weights[:, None, None] * weights[None, :, None] * weights[None, None, :]
    return derivative.astype(np.float32), weight_cube.astype(np.float32)


def derivative_matrices():
    derivative, weight_cube = gll_tables()
    eye = np.eye(5, dtype=np.float32)
    whole = np.zeros((3, LANES, LANES), np.float32)
    whole[0, :125, :125] = np.kron(derivative, np.kron(eye, eye))
    whole[1, :125, :125] = np.kron(eye, np.kron(derivative, eye))
    whole[2, :125, :125] = np.kron(eye, np.kron(eye, derivative))
    whole = whole.reshape(3 * LANES, LANES)
    high = whole.astype(jnp.bfloat16)
    low = (whole - high.astype(np.float32)).astype(jnp.bfloat16)
    weights = np.zeros((8, LANES), np.float32)
    weights[:, :125] = weight_cube.reshape(1, 125)
    return high, low, weights


def when(condition, action):
    if condition is None:
        action()
    else:
        pl.when(condition)(action)


def split(x):
    high = x.astype(bf16)
    return high, (x - high.astype(f32)).astype(bf16)


def dot(a, b, dims):
    return lax.dot_general(a, b, (dims, ((), ())), preferred_element_type=f32)


def dot_split(x, high, low, dims):
    x_high, x_low = split(x)
    return dot(x_high, high, dims) + dot(x_low, high, dims) + dot(x_high, low, dims)


def lookup(tables, hi, lo):
    out = [jnp.zeros(hi.shape, f32) for _ in tables]
    for h in range(len(tables[0])):
        here = hi == h
        for c, rows in enumerate(tables):
            picked = jnp.take_along_axis(
                jnp.broadcast_to(rows[h], hi.shape), lo, axis=1, mode="promise_in_bounds"
            )
            out[c] = jnp.where(here, picked, out[c])
    return out


def mark_low(marks_ref, lo):
    sublane = lax.broadcasted_iota(jnp.int32, (LANES, LANES), 0)
    for row in range(lo.shape[0]):
        line = jnp.broadcast_to(lo[row : row + 1], (LANES, LANES))
        marks_ref[:, row * LANES : (row + 1) * LANES] = jnp.where(line == sublane, 1.0, 0.0).astype(
            bf16
        )


def spread_high(terms_ref, hi, values):
    sublane = lax.broadcasted_iota(jnp.int32, (8, LANES), 0)
    parts = []
    for value in values:
        high = value.astype(bf16).astype(f32)
        parts.append((high, value - high))
    for row in range(hi.shape[0]):
        here = jnp.broadcast_to(hi[row : row + 1], (8, LANES)) == sublane
        for c, pair in enumerate(parts):
            both = [
                jnp.where(here, jnp.broadcast_to(part[row : row + 1], (8, LANES)), 0.0)
                for part in pair
            ]
            terms_ref[16 * c : 16 * c + 16, row * LANES : (row + 1) * LANES] = jnp.concatenate(
                both, axis=0
            ).astype(bf16)


def collect(terms_ref, marks_ref):
    sums = dot(terms_ref[...], marks_ref[...], ((1,), (1,)))
    return [
        sums[16 * c : 16 * c + 8] + sums[16 * c + 8 : 16 * c + 16]
        for c in range(terms_ref.shape[0] // 16)
    ]


def rows_of(ref, lead):
    line = ref[lead]
    return jnp.concatenate([line[:, LANES * t : LANES * (t + 1)] for t in range(8)], axis=0)


def both_sides(ref, *lead):
    return jnp.concatenate(
        [rows_of(ref, (*lead, slice(p, p + 1), slice(None))) for p in range(2)], axis=0
    )


def step_kernel(n_region, n_dom, n_inputs, *refs):
    sources = refs[:n_inputs]
    velocity_out, acceleration_out, dot_out, ddot_out = refs[n_inputs : n_inputs + 4]
    held = refs[n_inputs + 4 : 2 * n_inputs + 4]
    (
        load_sem,
        send_sem,
        recv_sem,
        motion_send,
        motion_recv,
        pressure_send,
        pressure_recv,
        fluid_send,
        fluid_recv,
        solid_send,
        solid_recv,
        index_pad,
        field_pad,
        fluid_index_pad,
        fluid_field_pad,
        element_terms,
        element_marks,
        fluid_terms,
        fluid_marks,
        slot_terms,
        slot_marks,
        arrived_terms,
        arrived_marks,
    ) = refs[2 * n_inputs + 4 :]
    (
        displacement,
        velocity,
        acceleration,
        solid_interface,
        interface_normal,
        potential,
        potential_dot,
        potential_ddot,
        fluid_connectivity,
        density_inverse,
        fluid_inverse_size,
        matrix_high,
        matrix_low,
        weight_cube,
        fluid_interface,
        fluid_halo,
        fluid_mass_inverse,
        connectivity,
        lame_lambda,
        shear_modulus,
        inverse_size,
        solid_halo,
        solid_mass_inverse,
    ) = held

    region, dom = lax.axis_index("region"), lax.axis_index("dom")
    above = (lax.rem(region + 1, n_region), dom)
    below = (lax.rem(region + n_region - 1, n_region), dom)
    upper = (region, lax.rem(dom + 1, n_dom))
    lower = (region, lax.rem(dom + n_dom - 1, n_dom))

    has_above, has_below = region < n_region - 1, region > 0
    for ref in (motion_recv, pressure_recv):
        ref[...] = jnp.zeros(ref.shape, f32)
    barrier = pltpu.get_barrier_semaphore()
    for held_if, other in ((has_above, above), (has_below, below), (None, upper), (None, lower)):
        when(
            held_if,
            lambda other=other: pl.semaphore_signal(
                barrier, inc=1, device_id=other, device_id_type=MESH
            ),
        )
    loads = [
        pltpu.make_async_copy(source, target, load_sem.at[i])
        for i, (source, target) in enumerate(zip(sources, held))
    ]
    for load in loads:
        load.start()

    def send(send_ref, recv_ref, flow, to_higher, to_lower, conditions=(None, None)):
        copies = []
        for side, target in ((0, to_higher), (1, to_lower)):
            copy = pltpu.make_async_remote_copy(
                src_ref=send_ref.at[side],
                dst_ref=recv_ref.at[side],
                send_sem=send_sem.at[2 * flow + side],
                recv_sem=recv_sem.at[2 * flow + side],
                device_id=target,
                device_id_type=MESH,
            )
            when(conditions[side], copy.start)
            copies.append((copy, conditions[side], conditions[1 - side]))
        return copies

    def receive(copies):
        for copy, _, condition in copies:
            when(condition, copy.wait_recv)

    ends = (has_above, has_below)

    for i in range(5):
        loads[i].wait()
    half_square = 0.5 * time_step * time_step
    predicted = displacement[...] + time_step * velocity[...] + half_square * acceleration[...]
    solid_tables = [
        [predicted[c : c + 1, LANES * h : LANES * (h + 1)] for h in range(8)] for c in range(3)
    ]
    slots = both_sides(solid_interface)
    slot_hi, slot_lo = slots >> 7, slots & 127
    normals = [both_sides(interface_normal, c) for c in range(3)]
    moved = lookup(solid_tables, slot_hi, slot_lo)
    motion = normals[0] * moved[0] + normals[1] * moved[1] + normals[2] * moved[2]
    motion_send[0] = motion[8:]
    motion_send[1] = motion[:8]
    peers = 2 + lax.div(region + n_region - 1, n_region)
    peers = peers + lax.div(2 * n_region - 2 - region, n_region)
    pl.semaphore_wait(barrier, peers)
    motion_copies = send(motion_send, motion_recv, 0, above, below, ends)

    for i in range(5, 14):
        loads[i].wait()
    fluid_predicted = (
        potential[...] + time_step * potential_dot[...] + half_square * potential_ddot[...]
    )
    fluid_table = [[fluid_predicted[h : h + 1] for h in range(4)]]
    fluid_index_pad[...] = jnp.full(fluid_index_pad.shape, -1, jnp.int32)
    fluid_index_pad[:, :125] = fluid_connectivity[...]
    fluid_field_pad[...] = jnp.zeros(fluid_field_pad.shape, f32)
    fluid_field_pad[:, :125] = density_inverse[...].astype(f32)
    fluid_index = fluid_index_pad[...]
    fluid_hi, fluid_lo = fluid_index >> 7, fluid_index & 127
    local = lookup(fluid_table, fluid_hi, fluid_lo)[0]
    high, low = matrix_high[...], matrix_low[...]
    gradient = dot_split(local, high, low, ((1,), (1,)))

    def column(line, count):
        rows = lax.broadcasted_iota(jnp.int32, (count, count), 0)
        columns = lax.broadcasted_iota(jnp.int32, (count, count), 1)
        wide = jnp.broadcast_to(line, (count, count))
        return jnp.sum(jnp.where(rows == columns, wide, 0.0), axis=1, keepdims=True)

    weights = weight_cube[0:1]
    fluid_factor = weights * fluid_field_pad[...] * (-1.0 / column(fluid_inverse_size[...], 16))
    weighted = jnp.concatenate(
        [gradient[:, LANES * b : LANES * (b + 1)] * fluid_factor for b in range(3)], axis=1
    )
    element = dot_split(weighted, high, low, ((1,), (0,)))
    mark_low(fluid_marks, fluid_lo)
    spread_high(fluid_terms, fluid_hi, [element])
    fluid_force = collect(fluid_terms, fluid_marks)[0]

    for i in range(14, 17):
        loads[i].wait()
    fluid_slots = both_sides(fluid_interface)
    arrived_hi, arrived_lo = fluid_slots >> 7, fluid_slots & 127
    mark_low(arrived_marks, arrived_lo)
    receive(motion_copies)
    spread_high(
        arrived_terms, arrived_hi, [jnp.concatenate([motion_recv[0], motion_recv[1]], axis=0)]
    )
    fluid_total = fluid_force + collect(arrived_terms, arrived_marks)[0]

    def rim_index(halo_ref, pad_ref, count):
        pad_ref[...] = jnp.full(pad_ref.shape, -1, jnp.int32)
        pad_ref[0:2, :count] = halo_ref[...]
        return pad_ref[...]

    fluid_rim = rim_index(fluid_halo, index_pad.at[0:8], 48)
    rim_values = lookup(
        [[fluid_total[h : h + 1] for h in range(4)]], fluid_rim >> 7, fluid_rim & 127
    )[0]
    fluid_send[0] = rim_values[1:2]
    fluid_send[1] = rim_values[0:1]
    fluid_copies = send(fluid_send, fluid_recv, 1, upper, lower)

    def slot_of_node(rim):
        out = []
        marks_lane = lax.broadcasted_iota(jnp.int32, (LANES, LANES), 0)
        sublane = lax.broadcasted_iota(jnp.int32, (8, LANES), 0)
        number = lax.broadcasted_iota(jnp.int32, (8, LANES), 1).astype(f32) + 1.0
        for side in range(2):
            line = rim[side : side + 1]
            marks = jnp.where(
                jnp.broadcast_to(line & 127, (LANES, LANES)) == marks_lane, 1.0, 0.0
            ).astype(bf16)
            terms = jnp.where(jnp.broadcast_to(line >> 7, (8, LANES)) == sublane, number, 0.0)
            out.append(dot(terms.astype(bf16), marks, ((1,), (1,))).astype(jnp.int32) - 1)
        return out

    def add_rims(total, arrived, places):
        for line, place in zip(arrived, places):
            picked = jnp.take_along_axis(
                jnp.broadcast_to(line, place.shape),
                jnp.maximum(place, 0),
                axis=1,
                mode="promise_in_bounds",
            )
            total = total + jnp.where(place >= 0, picked, 0.0)
        return total

    fluid_places = slot_of_node(fluid_rim)

    for i in range(17, 23):
        loads[i].wait()
    index_pad[...] = jnp.full(index_pad.shape, -1, jnp.int32)
    index_pad[:, :125] = connectivity[...]
    index = index_pad[...]
    hi, lo = index >> 7, index & 127
    values = lookup(solid_tables, hi, lo)
    gradient = dot_split(jnp.concatenate(values, axis=0), high, low, ((1,), (1,)))
    field_pad[...] = jnp.zeros(field_pad.shape, f32)
    field_pad[:, :125] = lame_lambda[...].astype(f32)
    lame = field_pad[...]
    field_pad[:, :125] = shear_modulus[...].astype(f32)
    shear = field_pad[...]
    factor = weights * (-1.0 / column(inverse_size[...], 32))
    lame, shear = lame * factor, shear * factor
    grad = [
        [gradient[32 * c : 32 * c + 32, LANES * b : LANES * (b + 1)] for b in range(3)]
        for c in range(3)
    ]
    trace = lame * (grad[0][0] + grad[1][1] + grad[2][2])
    stress = [[None] * 3 for _ in range(3)]
    for a in range(3):
        stress[a][a] = trace + shear * (grad[a][a] + grad[a][a])
        for b in range(a):
            stress[a][b] = stress[b][a] = shear * (grad[a][b] + grad[b][a])
    weighted = jnp.concatenate([jnp.concatenate(row, axis=1) for row in stress], axis=0)
    element = dot_split(weighted, high, low, ((1,), (0,)))
    mark_low(element_marks, lo)
    spread_high(element_terms, hi, [element[32 * c : 32 * c + 32] for c in range(3)])

    receive(fluid_copies)
    assembled = add_rims(fluid_total, [fluid_recv[0], fluid_recv[1]], fluid_places)
    ddot = fluid_mass_inverse[...] * assembled[:4]
    pressure = lookup([[ddot[h : h + 1] for h in range(4)]], arrived_hi, arrived_lo)[0]
    pressure_send[0] = pressure[8:]
    pressure_send[1] = pressure[:8]
    pressure_copies = send(pressure_send, pressure_recv, 2, above, below, ends)
    ddot_out[...] = ddot
    dot_out[...] = potential_dot[...] + 0.5 * time_step * (potential_ddot[...] + ddot)

    force = collect(element_terms, element_marks)
    mark_low(slot_marks, slot_lo)
    solid_rim = rim_index(solid_halo, index_pad.at[0:8], 96)
    solid_places = slot_of_node(solid_rim)
    receive(pressure_copies)
    arrived = jnp.concatenate([pressure_recv[0], pressure_recv[1]], axis=0)
    spread_high(slot_terms, slot_hi, [-(normal * arrived) for normal in normals])
    coupling = collect(slot_terms, slot_marks)
    total = [a + b for a, b in zip(force, coupling)]
    rim_values = lookup(
        [[t[h : h + 1] for h in range(8)] for t in total], solid_rim >> 7, solid_rim & 127
    )
    for c in range(3):
        solid_send[0, c : c + 1] = rim_values[c][1:2]
        solid_send[1, c : c + 1] = rim_values[c][0:1]
    solid_copies = send(solid_send, solid_recv, 3, upper, lower)
    mass = solid_mass_inverse[...]
    base = [
        rows_of(velocity, (slice(c, c + 1), slice(None)))
        + 0.5 * time_step * rows_of(acceleration, (slice(c, c + 1), slice(None)))
        for c in range(3)
    ]
    receive(solid_copies)
    for c in range(3):
        arrived = [solid_recv[side, c : c + 1] for side in range(2)]
        new = mass * add_rims(total[c], arrived, solid_places)
        speed = base[c] + 0.5 * time_step * new
        for h in range(8):
            acceleration_out[c : c + 1, LANES * h : LANES * (h + 1)] = new[h : h + 1]
            velocity_out[c : c + 1, LANES * h : LANES * (h + 1)] = speed[h : h + 1]
    for copy, condition, _ in motion_copies + fluid_copies + pressure_copies + solid_copies:
        when(condition, copy.wait_send)


def write_kernel(*refs):
    sem = refs[-1]
    copies = [
        pltpu.make_async_copy(refs[i], refs[4 + i], sem.at[i]) for i in range(4)
    ]
    for copy in copies:
        copy.start()
    for copy in copies:
        copy.wait()


def on_device(
    n_region,
    n_dom,
    displacement,
    velocity,
    acceleration,
    solid_mass_inverse,
    connectivity,
    lame_lambda,
    shear_modulus,
    inverse_size,
    potential,
    potential_dot,
    potential_ddot,
    fluid_mass_inverse,
    fluid_connectivity,
    density_inverse,
    fluid_inverse_size,
    solid_halo,
    fluid_halo,
    solid_interface,
    fluid_interface,
    interface_normal,
):
    high, low, weights = derivative_matrices()
    operands = (
        displacement,
        velocity,
        acceleration,
        solid_interface,
        interface_normal,
        potential.reshape(4, LANES),
        potential_dot.reshape(4, LANES),
        potential_ddot.reshape(4, LANES),
        fluid_connectivity.T,
        density_inverse.T,
        fluid_inverse_size.reshape(1, 16),
        jnp.asarray(high),
        jnp.asarray(low),
        jnp.asarray(weights),
        fluid_interface,
        fluid_halo,
        fluid_mass_inverse.reshape(4, LANES),
        connectivity.T,
        lame_lambda.T,
        shear_modulus.T,
        inverse_size.reshape(1, 32),
        solid_halo,
        solid_mass_inverse.reshape(8, LANES),
    )
    count = len(operands)
    vmem = pltpu.VMEM
    shapes = ((3, 1024), (3, 1024), (4, LANES), (4, LANES))
    outs = pl.pallas_call(
        lambda *refs: step_kernel(n_region, n_dom, count, *refs),
        out_shape=tuple(pltpu.VMEM(shape, f32) for shape in shapes),
        in_specs=[pl.BlockSpec(memory_space=pl.ANY)] * count,
        out_specs=[pl.BlockSpec(memory_space=vmem)] * 4,
        scratch_shapes=[vmem(x.shape, x.dtype) for x in operands]
        + [
            pltpu.SemaphoreType.DMA((count,)),
            pltpu.SemaphoreType.DMA((8,)),
            pltpu.SemaphoreType.DMA((8,)),
            vmem((2, 8, LANES), f32),
            vmem((2, 8, LANES), f32),
            vmem((2, 8, LANES), f32),
            vmem((2, 8, LANES), f32),
            vmem((2, 1, LANES), f32),
            vmem((2, 1, LANES), f32),
            vmem((2, 3, LANES), f32),
            vmem((2, 3, LANES), f32),
            vmem((32, LANES), jnp.int32),
            vmem((32, LANES), f32),
            vmem((16, LANES), jnp.int32),
            vmem((16, LANES), f32),
            vmem((48, 32 * LANES), bf16),
            vmem((LANES, 32 * LANES), bf16),
            vmem((16, 16 * LANES), bf16),
            vmem((LANES, 16 * LANES), bf16),
            vmem((48, 16 * LANES), bf16),
            vmem((LANES, 16 * LANES), bf16),
            vmem((16, 16 * LANES), bf16),
            vmem((LANES, 16 * LANES), bf16),
        ],
        compiler_params=pltpu.CompilerParams(collective_id=0, has_side_effects=True),
        name="newmark_step",
    )(*operands)
    outs = pl.pallas_call(
        write_kernel,
        out_shape=tuple(jax.ShapeDtypeStruct(shape, f32) for shape in shapes),
        in_specs=[pl.BlockSpec(memory_space=vmem)] * 4,
        out_specs=[pl.BlockSpec(memory_space=pl.ANY)] * 4,
        scratch_shapes=[pltpu.SemaphoreType.DMA((4,))],
        name="write_results",
    )(*[pltpu.with_memory_space_constraint(x, vmem) for x in outs])
    return outs[0], outs[1], outs[2].reshape(512), outs[3].reshape(512)


def solution(mesh):
    cut = ("region", "dom")
    line, plane = P(cut), P(None, cut)
    in_specs = (
        (plane,) * 3
        + (line,)
        + (plane,) * 3
        + (line,) * 5
        + (plane,) * 2
        + (line,)
        + (plane,) * 4
        + (P(None, None, cut),)
    )
    n_region, n_dom = mesh.shape["region"], mesh.shape["dom"]
    return jax.shard_map(
        lambda *args: on_device(n_region, n_dom, *args),
        mesh=mesh,
        in_specs=in_specs,
        out_specs=(plane, plane, line, line),
        check_vma=False,
    )
```

```python
import math

import jax
import jax.numpy as jnp
import numpy as np
from jax import lax
from jax.experimental import pallas as pl
from jax.experimental.pallas import tpu as pltpu
from jax.sharding import PartitionSpec as P

time_step = 0.4
MESH = pl.DeviceIdType.MESH
LANES = 128
f32 = jnp.float32
bf16 = jnp.bfloat16


def gll_tables():
    points = np.array([-1.0, -math.sqrt(3.0 / 7.0), 0.0, math.sqrt(3.0 / 7.0), 1.0])
    weights = np.array([0.1, 49.0 / 90.0, 32.0 / 45.0, 49.0 / 90.0, 0.1])
    products = np.array(
        [np.prod([points[i] - points[j] for j in range(5) if j != i]) for i in range(5)]
    )
    derivative = np.zeros((5, 5))
    for i in range(5):
        for j in range(5):
            if i != j:
                derivative[i, j] = products[i] / (products[j] * (points[i] - points[j]))
            else:
                derivative[i, j] = sum(1.0 / (points[i] - points[k]) for k in range(5) if k != i)
    weight_cube = weights[:, None, None] * weights[None, :, None] * weights[None, None, :]
    return derivative.astype(np.float32), weight_cube.astype(np.float32)


def derivative_matrices():
    derivative, weight_cube = gll_tables()
    eye = np.eye(5, dtype=np.float32)
    whole = np.zeros((3, LANES, LANES), np.float32)
    whole[0, :125, :125] = np.kron(derivative, np.kron(eye, eye))
    whole[1, :125, :125] = np.kron(eye, np.kron(derivative, eye))
    whole[2, :125, :125] = np.kron(eye, np.kron(eye, derivative))
    whole = whole.reshape(3 * LANES, LANES)
    high = whole.astype(jnp.bfloat16)
    low = (whole - high.astype(np.float32)).astype(jnp.bfloat16)
    weights = np.zeros((8, LANES), np.float32)
    weights[:, :125] = weight_cube.reshape(1, 125)
    return high, low, weights


def when(condition, action):
    if condition is None:
        action()
    else:
        pl.when(condition)(action)


def split(x):
    high = x.astype(bf16)
    return high, (x - high.astype(f32)).astype(bf16)


def dot(a, b, dims):
    return lax.dot_general(a, b, (dims, ((), ())), preferred_element_type=f32)


def dot_split(x, high, low, dims):
    x_high, x_low = split(x)
    return dot(x_high, high, dims) + dot(x_low, high, dims) + dot(x_high, low, dims)


def lookup(tables, hi, lo):
    out = [jnp.zeros(hi.shape, f32) for _ in tables]
    for h in range(len(tables[0])):
        here = hi == h
        for c, rows in enumerate(tables):
            picked = jnp.take_along_axis(
                jnp.broadcast_to(rows[h], hi.shape), lo, axis=1, mode="promise_in_bounds"
            )
            out[c] = jnp.where(here, picked, out[c])
    return out


def mark_low(marks_ref, lo):
    sublane = lax.broadcasted_iota(jnp.int32, (LANES, LANES), 0)
    for row in range(lo.shape[0]):
        line = jnp.broadcast_to(lo[row : row + 1], (LANES, LANES))
        marks_ref[:, row * LANES : (row + 1) * LANES] = jnp.where(line == sublane, 1.0, 0.0).astype(
            bf16
        )


def spread_high(terms_ref, hi, values):
    sublane = lax.broadcasted_iota(jnp.int32, (8, LANES), 0)
    parts = []
    for value in values:
        high = value.astype(bf16).astype(f32)
        parts.append((high, value - high))
    for row in range(hi.shape[0]):
        here = jnp.broadcast_to(hi[row : row + 1], (8, LANES)) == sublane
        for c, pair in enumerate(parts):
            both = [
                jnp.where(here, jnp.broadcast_to(part[row : row + 1], (8, LANES)), 0.0)
                for part in pair
            ]
            terms_ref[16 * c : 16 * c + 16, row * LANES : (row + 1) * LANES] = jnp.concatenate(
                both, axis=0
            ).astype(bf16)


def collect(terms_ref, marks_ref):
    sums = dot(terms_ref[...], marks_ref[...], ((1,), (1,)))
    return [
        sums[16 * c : 16 * c + 8] + sums[16 * c + 8 : 16 * c + 16]
        for c in range(terms_ref.shape[0] // 16)
    ]


def rows_of(ref, lead):
    line = ref[lead]
    return jnp.concatenate([line[:, LANES * t : LANES * (t + 1)] for t in range(8)], axis=0)


def both_sides(ref, *lead):
    return jnp.concatenate(
        [rows_of(ref, (*lead, slice(p, p + 1), slice(None))) for p in range(2)], axis=0
    )


def step_kernel(n_region, n_dom, n_inputs, *refs):
    sources = refs[:n_inputs]
    velocity_out, acceleration_out, dot_out, ddot_out = refs[n_inputs : n_inputs + 4]
    held = refs[n_inputs + 4 : 2 * n_inputs + 4]
    (
        load_sem,
        send_sem,
        recv_sem,
        motion_send,
        motion_recv,
        slot_send,
        slot_recv,
        static_send,
        static_recv,
        fluid_send,
        fluid_recv,
        solid_send,
        solid_recv,
        index_pad,
        field_pad,
        fluid_index_pad,
        fluid_field_pad,
        element_terms,
        element_marks,
        fluid_terms,
        fluid_marks,
        slot_terms,
        slot_marks,
        arrived_terms,
        arrived_marks,
    ) = refs[2 * n_inputs + 4 :]
    (
        displacement,
        velocity,
        acceleration,
        solid_interface,
        interface_normal,
        potential,
        potential_dot,
        potential_ddot,
        fluid_connectivity,
        density_inverse,
        fluid_inverse_size,
        matrix_high,
        matrix_low,
        weight_cube,
        fluid_interface,
        fluid_halo,
        fluid_mass_inverse,
        connectivity,
        lame_lambda,
        shear_modulus,
        inverse_size,
        solid_halo,
        solid_mass_inverse,
    ) = held

    region, dom = lax.axis_index("region"), lax.axis_index("dom")
    has_above, has_below = region < n_region - 1, region > 0
    to_region = {1: (has_above, has_below), -1: (has_below, has_above), 0: (None, None)}
    device = {
        (up, along): (
            region + up,
            lax.rem(dom + n_dom + along, n_dom),
        )
        for up in (-1, 0, 1)
        for along in (-1, 0, 1)
    }
    for ref in (motion_recv, slot_recv, static_recv, fluid_recv):
        ref[...] = jnp.zeros(ref.shape, f32)
    barrier = pltpu.get_barrier_semaphore()
    for (up, along), other in device.items():
        if (up, along) != (0, 0):
            when(
                to_region[up][0],
                lambda other=other: pl.semaphore_signal(
                    barrier, inc=1, device_id=other, device_id_type=MESH
                ),
            )
    loads = [
        pltpu.make_async_copy(source, target, load_sem.at[i])
        for i, (source, target) in enumerate(zip(sources, held))
    ]
    for load in loads:
        load.start()

    started = []

    def send(*messages):
        copies = []
        for source, target, up, along in messages:
            number = len(started)
            copy = pltpu.make_async_remote_copy(
                src_ref=source,
                dst_ref=target,
                send_sem=send_sem.at[number],
                recv_sem=recv_sem.at[number],
                device_id=device[up, along],
                device_id_type=MESH,
            )
            when(to_region[up][0], copy.start)
            started.append((copy, to_region[up][0]))
            copies.append((copy, to_region[up][1]))
        return copies

    def receive(copies):
        for copy, condition in copies:
            when(condition, copy.wait_recv)

    for i in range(5):
        loads[i].wait()
    half_square = 0.5 * time_step * time_step
    predicted = displacement[...] + time_step * velocity[...] + half_square * acceleration[...]
    solid_tables = [
        [predicted[c : c + 1, LANES * h : LANES * (h + 1)] for h in range(8)] for c in range(3)
    ]
    slots = both_sides(solid_interface)
    slot_hi, slot_lo = slots >> 7, slots & 127
    normals = [both_sides(interface_normal, c) for c in range(3)]
    moved = lookup(solid_tables, slot_hi, slot_lo)
    motion = normals[0] * moved[0] + normals[1] * moved[1] + normals[2] * moved[2]
    motion_send[0] = motion[8:]
    motion_send[1] = motion[:8]
    peers = 2 + 3 * lax.div(region + n_region - 1, n_region)
    peers = peers + 3 * lax.div(2 * n_region - 2 - region, n_region)
    pl.semaphore_wait(barrier, peers)
    motion_copies = send(
        (motion_send.at[0], motion_recv.at[0], 1, 0),
        (motion_send.at[1], motion_recv.at[1], -1, 0),
    )

    for i in range(5, 14):
        loads[i].wait()
    fluid_predicted = (
        potential[...] + time_step * potential_dot[...] + half_square * potential_ddot[...]
    )
    fluid_table = [[fluid_predicted[h : h + 1] for h in range(4)]]
    fluid_index_pad[...] = jnp.full(fluid_index_pad.shape, -1, jnp.int32)
    fluid_index_pad[:, :125] = fluid_connectivity[...]
    fluid_field_pad[...] = jnp.zeros(fluid_field_pad.shape, f32)
    fluid_field_pad[:, :125] = density_inverse[...].astype(f32)
    fluid_index = fluid_index_pad[...]
    fluid_hi, fluid_lo = fluid_index >> 7, fluid_index & 127
    local = lookup(fluid_table, fluid_hi, fluid_lo)[0]
    high, low = matrix_high[...], matrix_low[...]
    gradient = dot_split(local, high, low, ((1,), (1,)))

    def column(line, count):
        rows = lax.broadcasted_iota(jnp.int32, (count, count), 0)
        columns = lax.broadcasted_iota(jnp.int32, (count, count), 1)
        wide = jnp.broadcast_to(line, (count, count))
        return jnp.sum(jnp.where(rows == columns, wide, 0.0), axis=1, keepdims=True)

    weights = weight_cube[0:1]
    fluid_factor = weights * fluid_field_pad[...] * (-1.0 / column(fluid_inverse_size[...], 16))
    weighted = jnp.concatenate(
        [gradient[:, LANES * b : LANES * (b + 1)] * fluid_factor for b in range(3)], axis=1
    )
    element = dot_split(weighted, high, low, ((1,), (0,)))
    mark_low(fluid_marks, fluid_lo)
    spread_high(fluid_terms, fluid_hi, [element])
    fluid_force = collect(fluid_terms, fluid_marks)[0]

    def rim_index(halo_ref, pad_ref, count):
        pad_ref[...] = jnp.full(pad_ref.shape, -1, jnp.int32)
        pad_ref[0:2, :count] = halo_ref[...]
        return pad_ref[...]

    def slot_of_node(rim):
        out = []
        marks_lane = lax.broadcasted_iota(jnp.int32, (LANES, LANES), 0)
        sublane = lax.broadcasted_iota(jnp.int32, (8, LANES), 0)
        number = lax.broadcasted_iota(jnp.int32, (8, LANES), 1).astype(f32) + 1.0
        for side in range(2):
            line = rim[side : side + 1]
            marks = jnp.where(
                jnp.broadcast_to(line & 127, (LANES, LANES)) == marks_lane, 1.0, 0.0
            ).astype(bf16)
            terms = jnp.where(jnp.broadcast_to(line >> 7, (8, LANES)) == sublane, number, 0.0)
            out.append(dot(terms.astype(bf16), marks, ((1,), (1,))))
        return out

    def pick(line, place):
        index = jnp.maximum(place.astype(jnp.int32) - 1, 0)
        wide = jnp.broadcast_to(line, place.shape)
        picked = jnp.take_along_axis(wide, index, axis=1, mode="promise_in_bounds")
        return jnp.where(place > 0.5, picked, 0.0)

    for i in range(14, 17):
        loads[i].wait()
    fluid_slots = both_sides(fluid_interface)
    arrived_hi, arrived_lo = fluid_slots >> 7, fluid_slots & 127
    fluid_rim = rim_index(fluid_halo, index_pad.at[0:8], 48)
    fluid_places = slot_of_node(fluid_rim)
    slot_mass = lookup(
        [[fluid_mass_inverse[h : h + 1] for h in range(4)]]
        + [[place[h : h + 1] for h in range(4)] for place in fluid_places],
        arrived_hi,
        arrived_lo,
    )
    for i in range(3):
        static_send[0, 8 * i : 8 * i + 8] = slot_mass[i][8:]
        static_send[1, 8 * i : 8 * i + 8] = slot_mass[i][:8]
    static_copies = send(
        (static_send.at[0], static_recv.at[0], 1, 0),
        (static_send.at[1], static_recv.at[1], -1, 0),
    )
    mark_low(arrived_marks, arrived_lo)
    receive(motion_copies)
    spread_high(
        arrived_terms, arrived_hi, [jnp.concatenate([motion_recv[0], motion_recv[1]], axis=0)]
    )
    fluid_total = fluid_force + collect(arrived_terms, arrived_marks)[0]

    total_rows = [[fluid_total[h : h + 1] for h in range(4)]]
    at_slots = lookup(total_rows, arrived_hi, arrived_lo)[0]
    slot_send[0] = at_slots[8:]
    slot_send[1] = at_slots[:8]
    rim_values = lookup(total_rows, fluid_rim >> 7, fluid_rim & 127)[0]
    fluid_send[0] = rim_values[1:2]
    fluid_send[1] = rim_values[0:1]
    rim_copies = [
        send(*((fluid_send.at[i], fluid_recv.at[i, 1 + up], up, 1 - 2 * i) for i in range(2)))
        for up in (1, -1)
    ]
    slot_copies = send(
        (slot_send.at[0], slot_recv.at[0], 1, 0),
        (slot_send.at[1], slot_recv.at[1], -1, 0),
    )
    fluid_copies = send(*((fluid_send.at[i], fluid_recv.at[i, 1], 0, 1 - 2 * i) for i in range(2)))

    for i in range(17, 23):
        loads[i].wait()
    index_pad[...] = jnp.full(index_pad.shape, -1, jnp.int32)
    index_pad[:, :125] = connectivity[...]
    index = index_pad[...]
    hi, lo = index >> 7, index & 127
    values = lookup(solid_tables, hi, lo)
    gradient = dot_split(jnp.concatenate(values, axis=0), high, low, ((1,), (1,)))
    field_pad[...] = jnp.zeros(field_pad.shape, f32)
    field_pad[:, :125] = lame_lambda[...].astype(f32)
    lame = field_pad[...]
    field_pad[:, :125] = shear_modulus[...].astype(f32)
    shear = field_pad[...]
    factor = weights * (-1.0 / column(inverse_size[...], 32))
    lame, shear = lame * factor, shear * factor
    grad = [
        [gradient[32 * c : 32 * c + 32, LANES * b : LANES * (b + 1)] for b in range(3)]
        for c in range(3)
    ]
    trace = lame * (grad[0][0] + grad[1][1] + grad[2][2])
    stress = [[None] * 3 for _ in range(3)]
    for a in range(3):
        stress[a][a] = trace + shear * (grad[a][a] + grad[a][a])
        for b in range(a):
            stress[a][b] = stress[b][a] = shear * (grad[a][b] + grad[b][a])
    weighted = jnp.concatenate([jnp.concatenate(row, axis=1) for row in stress], axis=0)
    element = dot_split(weighted, high, low, ((1,), (0,)))
    mark_low(element_marks, lo)
    spread_high(element_terms, hi, [element[32 * c : 32 * c + 32] for c in range(3)])

    force = collect(element_terms, element_marks)
    mark_low(slot_marks, slot_lo)
    solid_rim = rim_index(solid_halo, index_pad.at[0:8], 96)
    solid_places = slot_of_node(solid_rim)

    receive(fluid_copies)
    assembled = fluid_total
    for i in range(2):
        assembled = assembled + pick(fluid_recv[i, 1], fluid_places[i])
    ddot = fluid_mass_inverse[...] * assembled[:4]
    ddot_out[...] = ddot
    dot_out[...] = potential_dot[...] + 0.5 * time_step * (potential_ddot[...] + ddot)

    receive(static_copies)
    for copies in rim_copies:
        receive(copies)
    receive(slot_copies)
    arrived = []
    for i, source in ((0, 2), (1, 0)):
        mass, below_place, above_place = (static_recv[i, 8 * j : 8 * j + 8] for j in range(3))
        value = slot_recv[i] + pick(fluid_recv[0, source], below_place)
        arrived.append(mass * (value + pick(fluid_recv[1, source], above_place)))
    arrived = jnp.concatenate(arrived, axis=0)
    spread_high(slot_terms, slot_hi, [-(normal * arrived) for normal in normals])
    coupling = collect(slot_terms, slot_marks)
    total = [a + b for a, b in zip(force, coupling)]
    rim_values = lookup(
        [[t[h : h + 1] for h in range(8)] for t in total], solid_rim >> 7, solid_rim & 127
    )
    for c in range(3):
        solid_send[0, c : c + 1] = rim_values[c][1:2]
        solid_send[1, c : c + 1] = rim_values[c][0:1]
    solid_copies = send(
        (solid_send.at[0], solid_recv.at[0], 0, 1),
        (solid_send.at[1], solid_recv.at[1], 0, -1),
    )
    mass = solid_mass_inverse[...]
    base = [
        rows_of(velocity, (slice(c, c + 1), slice(None)))
        + 0.5 * time_step * rows_of(acceleration, (slice(c, c + 1), slice(None)))
        for c in range(3)
    ]
    receive(solid_copies)
    for c in range(3):
        assembled = total[c]
        for side in range(2):
            assembled = assembled + pick(solid_recv[side, c : c + 1], solid_places[side])
        new = mass * assembled
        speed = base[c] + 0.5 * time_step * new
        for h in range(8):
            acceleration_out[c : c + 1, LANES * h : LANES * (h + 1)] = new[h : h + 1]
            velocity_out[c : c + 1, LANES * h : LANES * (h + 1)] = speed[h : h + 1]
    for copy, condition in started:
        when(condition, copy.wait_send)


def write_kernel(*refs):
    sem = refs[-1]
    copies = [
        pltpu.make_async_copy(refs[i], refs[4 + i], sem.at[i]) for i in range(4)
    ]
    for copy in copies:
        copy.start()
    for copy in copies:
        copy.wait()


def on_device(
    n_region,
    n_dom,
    displacement,
    velocity,
    acceleration,
    solid_mass_inverse,
    connectivity,
    lame_lambda,
    shear_modulus,
    inverse_size,
    potential,
    potential_dot,
    potential_ddot,
    fluid_mass_inverse,
    fluid_connectivity,
    density_inverse,
    fluid_inverse_size,
    solid_halo,
    fluid_halo,
    solid_interface,
    fluid_interface,
    interface_normal,
):
    high, low, weights = derivative_matrices()
    operands = (
        displacement,
        velocity,
        acceleration,
        solid_interface,
        interface_normal,
        potential.reshape(4, LANES),
        potential_dot.reshape(4, LANES),
        potential_ddot.reshape(4, LANES),
        fluid_connectivity.T,
        density_inverse.T,
        fluid_inverse_size.reshape(1, 16),
        jnp.asarray(high),
        jnp.asarray(low),
        jnp.asarray(weights),
        fluid_interface,
        fluid_halo,
        fluid_mass_inverse.reshape(4, LANES),
        connectivity.T,
        lame_lambda.T,
        shear_modulus.T,
        inverse_size.reshape(1, 32),
        solid_halo,
        solid_mass_inverse.reshape(8, LANES),
    )
    count = len(operands)
    vmem = pltpu.VMEM
    shapes = ((3, 1024), (3, 1024), (4, LANES), (4, LANES))
    outs = pl.pallas_call(
        lambda *refs: step_kernel(n_region, n_dom, count, *refs),
        out_shape=tuple(pltpu.VMEM(shape, f32) for shape in shapes),
        in_specs=[pl.BlockSpec(memory_space=pl.ANY)] * count,
        out_specs=[pl.BlockSpec(memory_space=vmem)] * 4,
        scratch_shapes=[vmem(x.shape, x.dtype) for x in operands]
        + [
            pltpu.SemaphoreType.DMA((count,)),
            pltpu.SemaphoreType.DMA((14,)),
            pltpu.SemaphoreType.DMA((14,)),
            vmem((2, 8, LANES), f32),
            vmem((2, 8, LANES), f32),
            vmem((2, 8, LANES), f32),
            vmem((2, 8, LANES), f32),
            vmem((2, 24, LANES), f32),
            vmem((2, 24, LANES), f32),
            vmem((2, 1, LANES), f32),
            vmem((2, 3, 1, LANES), f32),
            vmem((2, 3, LANES), f32),
            vmem((2, 3, LANES), f32),
            vmem((32, LANES), jnp.int32),
            vmem((32, LANES), f32),
            vmem((16, LANES), jnp.int32),
            vmem((16, LANES), f32),
            vmem((48, 32 * LANES), bf16),
            vmem((LANES, 32 * LANES), bf16),
            vmem((16, 16 * LANES), bf16),
            vmem((LANES, 16 * LANES), bf16),
            vmem((48, 16 * LANES), bf16),
            vmem((LANES, 16 * LANES), bf16),
            vmem((16, 16 * LANES), bf16),
            vmem((LANES, 16 * LANES), bf16),
        ],
        compiler_params=pltpu.CompilerParams(collective_id=0, has_side_effects=True),
        name="newmark_step",
    )(*operands)
    outs = pl.pallas_call(
        write_kernel,
        out_shape=tuple(jax.ShapeDtypeStruct(shape, f32) for shape in shapes),
        in_specs=[pl.BlockSpec(memory_space=vmem)] * 4,
        out_specs=[pl.BlockSpec(memory_space=pl.ANY)] * 4,
        scratch_shapes=[pltpu.SemaphoreType.DMA((4,))],
        name="write_results",
    )(*[pltpu.with_memory_space_constraint(x, vmem) for x in outs])
    return outs[0], outs[1], outs[2].reshape(512), outs[3].reshape(512)


def solution(mesh):
    cut = ("region", "dom")
    line, plane = P(cut), P(None, cut)
    in_specs = (
        (plane,) * 3
        + (line,)
        + (plane,) * 3
        + (line,) * 5
        + (plane,) * 2
        + (line,)
        + (plane,) * 4
        + (P(None, None, cut),)
    )
    n_region, n_dom = mesh.shape["region"], mesh.shape["dom"]
    return jax.shard_map(
        lambda *args: on_device(n_region, n_dom, *args),
        mesh=mesh,
        in_specs=in_specs,
        out_specs=(plane, plane, line, line),
        check_vma=False,
    )
```

```python
import math

import jax
import jax.numpy as jnp
import numpy as np
from jax import lax
from jax.experimental import pallas as pl
from jax.experimental.pallas import tpu as pltpu
from jax.sharding import PartitionSpec as P

time_step = 0.4
MESH = pl.DeviceIdType.MESH
LANES = 128
f32 = jnp.float32
bf16 = jnp.bfloat16


def gll_tables():
    points = np.array([-1.0, -math.sqrt(3.0 / 7.0), 0.0, math.sqrt(3.0 / 7.0), 1.0])
    weights = np.array([0.1, 49.0 / 90.0, 32.0 / 45.0, 49.0 / 90.0, 0.1])
    products = np.array(
        [np.prod([points[i] - points[j] for j in range(5) if j != i]) for i in range(5)]
    )
    derivative = np.zeros((5, 5))
    for i in range(5):
        for j in range(5):
            if i != j:
                derivative[i, j] = products[i] / (products[j] * (points[i] - points[j]))
            else:
                derivative[i, j] = sum(1.0 / (points[i] - points[k]) for k in range(5) if k != i)
    weight_cube = weights[:, None, None] * weights[None, :, None] * weights[None, None, :]
    return derivative.astype(np.float32), weight_cube.astype(np.float32)


def derivative_matrices():
    derivative, weight_cube = gll_tables()
    eye = np.eye(5, dtype=np.float32)
    whole = np.zeros((3, LANES, LANES), np.float32)
    whole[0, :125, :125] = np.kron(derivative, np.kron(eye, eye))
    whole[1, :125, :125] = np.kron(eye, np.kron(derivative, eye))
    whole[2, :125, :125] = np.kron(eye, np.kron(eye, derivative))
    whole = whole.reshape(3 * LANES, LANES)
    high = whole.astype(jnp.bfloat16)
    low = (whole - high.astype(np.float32)).astype(jnp.bfloat16)
    weights = np.zeros((8, LANES), np.float32)
    weights[:, :125] = weight_cube.reshape(1, 125)
    return high, low, weights


def when(condition, action):
    if condition is None:
        action()
    else:
        pl.when(condition)(action)


def split(x):
    high = x.astype(bf16)
    return high, (x - high.astype(f32)).astype(bf16)


def dot(a, b, dims):
    return lax.dot_general(a, b, (dims, ((), ())), preferred_element_type=f32)


def dot_split(x, high, low, dims):
    x_high, x_low = split(x)
    return dot(x_high, high, dims) + dot(x_low, high, dims) + dot(x_high, low, dims)


def lookup(tables, hi, lo):
    out = [jnp.zeros(hi.shape, f32) for _ in tables]
    for h in range(len(tables[0])):
        here = hi == h
        for c, rows in enumerate(tables):
            picked = jnp.take_along_axis(
                jnp.broadcast_to(rows[h], hi.shape), lo, axis=1, mode="promise_in_bounds"
            )
            out[c] = jnp.where(here, picked, out[c])
    return out


def mark_low(marks_ref, lo):
    sublane = lax.broadcasted_iota(jnp.int32, (LANES, LANES), 0)
    for row in range(lo.shape[0]):
        line = jnp.broadcast_to(lo[row : row + 1], (LANES, LANES))
        marks_ref[:, row * LANES : (row + 1) * LANES] = jnp.where(line == sublane, 1.0, 0.0).astype(
            bf16
        )


def spread_high(terms_ref, hi, values):
    sublane = lax.broadcasted_iota(jnp.int32, (8, LANES), 0)
    parts = []
    for value in values:
        high = value.astype(bf16).astype(f32)
        parts.append((high, value - high))
    for row in range(hi.shape[0]):
        here = jnp.broadcast_to(hi[row : row + 1], (8, LANES)) == sublane
        for c, pair in enumerate(parts):
            both = [
                jnp.where(here, jnp.broadcast_to(part[row : row + 1], (8, LANES)), 0.0)
                for part in pair
            ]
            terms_ref[16 * c : 16 * c + 16, row * LANES : (row + 1) * LANES] = jnp.concatenate(
                both, axis=0
            ).astype(bf16)


def collect(terms_ref, marks_ref):
    sums = dot(terms_ref[...], marks_ref[...], ((1,), (1,)))
    return [
        sums[16 * c : 16 * c + 8] + sums[16 * c + 8 : 16 * c + 16]
        for c in range(terms_ref.shape[0] // 16)
    ]


def spread_rows(terms_ref, values):
    sublane = lax.broadcasted_iota(jnp.int32, (8, LANES), 0)
    for c, value in enumerate(values):
        high = value.astype(bf16).astype(f32)
        pair = (high, value - high)
        for row in range(value.shape[0]):
            first = row // 8 * 8
            both = [
                jnp.where(sublane == row % 8, part[first : first + 8], 0.0) for part in pair
            ]
            terms_ref[16 * c : 16 * c + 16, row * LANES : (row + 1) * LANES] = jnp.concatenate(
                both, axis=0
            ).astype(bf16)


def rows_of(ref, lead):
    line = ref[lead]
    return jnp.concatenate([line[:, LANES * t : LANES * (t + 1)] for t in range(8)], axis=0)


def both_sides(ref, *lead):
    return jnp.concatenate(
        [rows_of(ref, (*lead, slice(p, p + 1), slice(None))) for p in range(2)], axis=0
    )


def step_kernel(n_region, n_dom, n_inputs, *refs):
    sources = refs[:n_inputs]
    velocity_out, acceleration_out, dot_out, ddot_out = refs[n_inputs : n_inputs + 4]
    held = refs[n_inputs + 4 : 2 * n_inputs + 4]
    (
        load_sem,
        send_sem,
        recv_sem,
        motion_send,
        motion_recv,
        static_send,
        static_recv,
        normals_send,
        normals_recv,
        rims_send,
        rims_recv,
        block_send,
        block_recv,
        fluid_send,
        fluid_recv,
        far_recv,
        index_pad,
        field_pad,
        fluid_index_pad,
        fluid_field_pad,
        element_terms,
        element_marks,
        fluid_terms,
        fluid_marks,
        slot_terms,
        slot_marks,
        arrived_terms,
        arrived_marks,
        near_terms,
        near_marks,
    ) = refs[2 * n_inputs + 4 :]
    (
        displacement,
        velocity,
        acceleration,
        solid_interface,
        interface_normal,
        potential,
        potential_dot,
        potential_ddot,
        fluid_connectivity,
        density_inverse,
        fluid_inverse_size,
        matrix_high,
        matrix_low,
        weight_cube,
        fluid_interface,
        fluid_halo,
        fluid_mass_inverse,
        connectivity,
        lame_lambda,
        shear_modulus,
        inverse_size,
        solid_halo,
        solid_mass_inverse,
    ) = held

    region, dom = lax.axis_index("region"), lax.axis_index("dom")
    has_above, has_below = region < n_region - 1, region > 0
    to_region = {1: (has_above, has_below), -1: (has_below, has_above), 0: (None, None)}
    device = {
        (up, along): (
            region + up,
            lax.rem(dom + n_dom + along, n_dom),
        )
        for up in (-1, 0, 1)
        for along in (-2, -1, 0, 1, 2)
    }
    for ref in (motion_recv, static_recv, block_recv, far_recv):
        ref[...] = jnp.zeros(ref.shape, f32)
    barrier = pltpu.get_barrier_semaphore()
    for (up, along), other in device.items():
        if up != 0 or along in (-1, 1):
            when(
                to_region[up][0],
                lambda other=other: pl.semaphore_signal(
                    barrier, inc=1, device_id=other, device_id_type=MESH
                ),
            )
    loads = [
        pltpu.make_async_copy(source, target, load_sem.at[i])
        for i, (source, target) in enumerate(zip(sources, held))
    ]
    for load in loads:
        load.start()

    started = []

    def send(*messages):
        copies = []
        for source, target, up, along in messages:
            number = len(started)
            copy = pltpu.make_async_remote_copy(
                src_ref=source,
                dst_ref=target,
                send_sem=send_sem.at[number],
                recv_sem=recv_sem.at[number],
                device_id=device[up, along],
                device_id_type=MESH,
            )
            when(to_region[up][0], copy.start)
            started.append((copy, to_region[up][0]))
            copies.append((copy, to_region[up][1]))
        return copies

    def receive(copies):
        for copy, condition in copies:
            when(condition, copy.wait_recv)

    for i in range(5):
        loads[i].wait()
    half_square = 0.5 * time_step * time_step
    predicted = displacement[...] + time_step * velocity[...] + half_square * acceleration[...]
    solid_tables = [
        [predicted[c : c + 1, LANES * h : LANES * (h + 1)] for h in range(8)] for c in range(3)
    ]
    slots = both_sides(solid_interface)
    slot_hi, slot_lo = slots >> 7, slots & 127
    normals = [both_sides(interface_normal, c) for c in range(3)]
    moved = lookup(solid_tables, slot_hi, slot_lo)
    motion = normals[0] * moved[0] + normals[1] * moved[1] + normals[2] * moved[2]
    motion_send[0] = motion[8:]
    motion_send[1] = motion[:8]

    for i in range(5, 14):
        loads[i].wait()
    fluid_predicted = (
        potential[...] + time_step * potential_dot[...] + half_square * potential_ddot[...]
    )
    fluid_table = [[fluid_predicted[h : h + 1] for h in range(4)]]
    fluid_index_pad[...] = jnp.full(fluid_index_pad.shape, -1, jnp.int32)
    fluid_index_pad[:, :125] = fluid_connectivity[...]
    fluid_field_pad[...] = jnp.zeros(fluid_field_pad.shape, f32)
    fluid_field_pad[:, :125] = density_inverse[...].astype(f32)
    fluid_index = fluid_index_pad[...]
    fluid_hi, fluid_lo = fluid_index >> 7, fluid_index & 127
    local = lookup(fluid_table, fluid_hi, fluid_lo)[0]
    high, low = matrix_high[...], matrix_low[...]
    gradient = dot_split(local, high, low, ((1,), (1,)))

    def column(line, count):
        rows = lax.broadcasted_iota(jnp.int32, (count, count), 0)
        columns = lax.broadcasted_iota(jnp.int32, (count, count), 1)
        wide = jnp.broadcast_to(line, (count, count))
        return jnp.sum(jnp.where(rows == columns, wide, 0.0), axis=1, keepdims=True)

    weights = weight_cube[0:1]
    fluid_factor = weights * fluid_field_pad[...] * (-1.0 / column(fluid_inverse_size[...], 16))
    weighted = jnp.concatenate(
        [gradient[:, LANES * b : LANES * (b + 1)] * fluid_factor for b in range(3)], axis=1
    )
    element = dot_split(weighted, high, low, ((1,), (0,)))
    mark_low(fluid_marks, fluid_lo)
    spread_high(fluid_terms, fluid_hi, [element])
    fluid_force = collect(fluid_terms, fluid_marks)[0]

    def rim_index(halo_ref, pad_ref, count):
        pad_ref[...] = jnp.full(pad_ref.shape, -1, jnp.int32)
        pad_ref[0:2, :count] = halo_ref[...]
        return pad_ref[...]

    def slot_of_node(rim):
        out = []
        marks_lane = lax.broadcasted_iota(jnp.int32, (LANES, LANES), 0)
        sublane = lax.broadcasted_iota(jnp.int32, (8, LANES), 0)
        number = lax.broadcasted_iota(jnp.int32, (8, LANES), 1).astype(f32) + 1.0
        for side in range(2):
            line = rim[side : side + 1]
            marks = jnp.where(
                jnp.broadcast_to(line & 127, (LANES, LANES)) == marks_lane, 1.0, 0.0
            ).astype(bf16)
            terms = jnp.where(jnp.broadcast_to(line >> 7, (8, LANES)) == sublane, number, 0.0)
            out.append(dot(terms.astype(bf16), marks, ((1,), (1,))))
        return out

    def pick(line, place):
        index = jnp.maximum(place.astype(jnp.int32) - 1, 0)
        wide = jnp.broadcast_to(line, place.shape)
        picked = jnp.take_along_axis(wide, index, axis=1, mode="promise_in_bounds")
        return jnp.where(place > 0.5, picked, 0.0)

    for i in range(14, 17):
        loads[i].wait()
    fluid_slots = both_sides(fluid_interface)
    arrived_hi, arrived_lo = fluid_slots >> 7, fluid_slots & 127
    fluid_rim = rim_index(fluid_halo, index_pad.at[0:8], 48)
    fluid_places = slot_of_node(fluid_rim)
    slot_mass = lookup(
        [[fluid_mass_inverse[h : h + 1] for h in range(4)]]
        + [[place[h : h + 1] for h in range(4)] for place in fluid_places],
        arrived_hi,
        arrived_lo,
    )
    for i in range(3):
        static_send[0, 8 * i : 8 * i + 8] = slot_mass[i][8:]
        static_send[1, 8 * i : 8 * i + 8] = slot_mass[i][:8]
    loads[21].wait()
    solid_rim = rim_index(solid_halo, index_pad.at[0:8], 96)
    solid_places = slot_of_node(solid_rim)
    slot_places = lookup(
        [[place[h : h + 1] for h in range(8)] for place in solid_places], slot_hi, slot_lo
    )
    for side in range(2):
        for c in range(3):
            normals_send[side, 16 * c : 16 * c + 16] = -normals[c]
        normals_send[side, 48:] = slot_places[1 - side]

    peers = 2 + 5 * lax.div(region + n_region - 1, n_region)
    peers = peers + 5 * lax.div(2 * n_region - 2 - region, n_region)
    pl.semaphore_wait(barrier, peers)
    motion_copies = send(
        (motion_send.at[0], motion_recv.at[0], 1, 0),
        (motion_send.at[1], motion_recv.at[1], -1, 0),
    )
    normals_copies = send(
        *((normals_send.at[i], normals_recv.at[i], 0, 1 - 2 * i) for i in range(2))
    )
    static_copies = send(
        *(
            (static_send.at[i], static_recv.at[i, 1 + along], 1 - 2 * i, along)
            for along in (-1, 0, 1)
            for i in range(2)
        )
    )

    for i in (17, 18, 19, 20, 22):
        loads[i].wait()
    index_pad[...] = jnp.full(index_pad.shape, -1, jnp.int32)
    index_pad[:, :125] = connectivity[...]
    index = index_pad[...]
    hi, lo = index >> 7, index & 127
    values = lookup(solid_tables, hi, lo)
    gradient = dot_split(jnp.concatenate(values, axis=0), high, low, ((1,), (1,)))
    field_pad[...] = jnp.zeros(field_pad.shape, f32)
    field_pad[:, :125] = lame_lambda[...].astype(f32)
    lame = field_pad[...]
    field_pad[:, :125] = shear_modulus[...].astype(f32)
    shear = field_pad[...]
    factor = weights * (-1.0 / column(inverse_size[...], 32))
    lame, shear = lame * factor, shear * factor
    grad = [
        [gradient[32 * c : 32 * c + 32, LANES * b : LANES * (b + 1)] for b in range(3)]
        for c in range(3)
    ]
    trace = lame * (grad[0][0] + grad[1][1] + grad[2][2])
    stress = [[None] * 3 for _ in range(3)]
    for a in range(3):
        stress[a][a] = trace + shear * (grad[a][a] + grad[a][a])
        for b in range(a):
            stress[a][b] = stress[b][a] = shear * (grad[a][b] + grad[b][a])
    weighted = jnp.concatenate([jnp.concatenate(row, axis=1) for row in stress], axis=0)
    element = dot_split(weighted, high, low, ((1,), (0,)))
    mark_low(element_marks, lo)
    spread_high(element_terms, hi, [element[32 * c : 32 * c + 32] for c in range(3)])

    force = collect(element_terms, element_marks)
    rim_values = lookup(
        [[t[h : h + 1] for h in range(8)] for t in force], solid_rim >> 7, solid_rim & 127
    )
    for c in range(3):
        rims_send[0, c : c + 1] = rim_values[c][1:2]
        rims_send[1, c : c + 1] = rim_values[c][0:1]
    rims_copies = send(*((rims_send.at[i], rims_recv.at[i], 0, 1 - 2 * i) for i in range(2)))
    mark_low(arrived_marks, arrived_lo)

    receive(motion_copies)
    spread_high(
        arrived_terms, arrived_hi, [jnp.concatenate([motion_recv[0], motion_recv[1]], axis=0)]
    )
    fluid_total = fluid_force + collect(arrived_terms, arrived_marks)[0]
    total_rows = [[fluid_total[h : h + 1] for h in range(4)]]
    at_slots = lookup(total_rows, arrived_hi, arrived_lo)[0]
    rim_values = lookup(total_rows, fluid_rim >> 7, fluid_rim & 127)[0]
    for i in range(2):
        block_send[i, :8] = at_slots[8 - 8 * i : 16 - 8 * i]
        block_send[i, 8:9] = rim_values[1:2]
        block_send[i, 9:10] = rim_values[0:1]
        fluid_send[i] = rim_values[1 - i : 2 - i]
    block_copies = send(
        *(
            (block_send.at[i], block_recv.at[i, 1 + along], 1 - 2 * i, along)
            for along in (-1, 1, 0)
            for i in range(2)
        ),
        *(
            (fluid_send.at[j], far_recv.at[i, j], 1 - 2 * i, 2 - 4 * j)
            for j in range(2)
            for i in range(2)
        ),
    )
    fluid_copies = send(*((fluid_send.at[i], fluid_recv.at[i], 0, 1 - 2 * i) for i in range(2)))

    mark_low(slot_marks, slot_lo)
    receive(normals_copies)
    for i in range(2):
        mark_low(near_marks.at[i], normals_recv[i, 48:].astype(jnp.int32) - 1)
    mass = solid_mass_inverse[...]
    base = [
        rows_of(velocity, (slice(c, c + 1), slice(None)))
        + 0.5 * time_step * rows_of(acceleration, (slice(c, c + 1), slice(None)))
        for c in range(3)
    ]
    receive(fluid_copies)
    assembled = fluid_total
    for i in range(2):
        assembled = assembled + pick(fluid_recv[i], fluid_places[i])
    ddot = fluid_mass_inverse[...] * assembled[:4]
    ddot_out[...] = ddot
    dot_out[...] = potential_dot[...] + 0.5 * time_step * (potential_ddot[...] + ddot)
    receive(static_copies)
    receive(rims_copies)

    receive(block_copies)

    def pressure_of(column):
        sides = []
        for i in range(2):
            block = block_recv.at[i, 1 - column]
            if column == -1:
                low_rim = far_recv[i, 0]
            else:
                low_rim = block_recv[i, 2 - column, 8:9]
            if column == 1:
                high_rim = far_recv[i, 1]
            else:
                high_rim = block_recv[i, -column, 9:10]
            slot_mass, low_place, high_place = (
                static_recv[i, 1 - column, 8 * j : 8 * j + 8] for j in range(3)
            )
            value = block[:8] + pick(low_rim, low_place)
            sides.append(slot_mass * (value + pick(high_rim, high_place)))
        return jnp.concatenate(sides, axis=0)

    arrived = pressure_of(0)
    spread_high(slot_terms, slot_hi, [-(normal * arrived) for normal in normals])
    for i in range(2):
        arrived = pressure_of(2 * i - 1)
        spread_rows(
            near_terms.at[i],
            [normals_recv[i, 16 * c : 16 * c + 16] * arrived for c in range(3)],
        )
    coupling = collect(slot_terms, slot_marks)
    near = []
    for i in range(2):
        sums = dot(near_terms[i], near_marks[i], ((1,), (1,)))
        near.append(
            [jnp.sum(sums[16 * c : 16 * c + 16], axis=0, keepdims=True) for c in range(3)]
        )
    for c in range(3):
        assembled = force[c] + coupling[c]
        for i in range(2):
            line = rims_recv[i, c : c + 1] + near[i][c]
            assembled = assembled + pick(line, solid_places[i])
        new = mass * assembled
        speed = base[c] + 0.5 * time_step * new
        for h in range(8):
            acceleration_out[c : c + 1, LANES * h : LANES * (h + 1)] = new[h : h + 1]
            velocity_out[c : c + 1, LANES * h : LANES * (h + 1)] = speed[h : h + 1]
    for copy, condition in started:
        when(condition, copy.wait_send)


def write_kernel(*refs):
    sem = refs[-1]
    copies = [
        pltpu.make_async_copy(refs[i], refs[4 + i], sem.at[i]) for i in range(4)
    ]
    for copy in copies:
        copy.start()
    for copy in copies:
        copy.wait()


def on_device(
    n_region,
    n_dom,
    displacement,
    velocity,
    acceleration,
    solid_mass_inverse,
    connectivity,
    lame_lambda,
    shear_modulus,
    inverse_size,
    potential,
    potential_dot,
    potential_ddot,
    fluid_mass_inverse,
    fluid_connectivity,
    density_inverse,
    fluid_inverse_size,
    solid_halo,
    fluid_halo,
    solid_interface,
    fluid_interface,
    interface_normal,
):
    high, low, weights = derivative_matrices()
    operands = (
        displacement,
        velocity,
        acceleration,
        solid_interface,
        interface_normal,
        potential.reshape(4, LANES),
        potential_dot.reshape(4, LANES),
        potential_ddot.reshape(4, LANES),
        fluid_connectivity.T,
        density_inverse.T,
        fluid_inverse_size.reshape(1, 16),
        jnp.asarray(high),
        jnp.asarray(low),
        jnp.asarray(weights),
        fluid_interface,
        fluid_halo,
        fluid_mass_inverse.reshape(4, LANES),
        connectivity.T,
        lame_lambda.T,
        shear_modulus.T,
        inverse_size.reshape(1, 32),
        solid_halo,
        solid_mass_inverse.reshape(8, LANES),
    )
    count = len(operands)
    vmem = pltpu.VMEM
    shapes = ((3, 1024), (3, 1024), (4, LANES), (4, LANES))
    outs = pl.pallas_call(
        lambda *refs: step_kernel(n_region, n_dom, count, *refs),
        out_shape=tuple(pltpu.VMEM(shape, f32) for shape in shapes),
        in_specs=[pl.BlockSpec(memory_space=pl.ANY)] * count,
        out_specs=[pl.BlockSpec(memory_space=vmem)] * 4,
        scratch_shapes=[vmem(x.shape, x.dtype) for x in operands]
        + [
            pltpu.SemaphoreType.DMA((count,)),
            pltpu.SemaphoreType.DMA((24,)),
            pltpu.SemaphoreType.DMA((24,)),
            vmem((2, 8, LANES), f32),
            vmem((2, 8, LANES), f32),
            vmem((2, 24, LANES), f32),
            vmem((2, 3, 24, LANES), f32),
            vmem((2, 64, LANES), f32),
            vmem((2, 64, LANES), f32),
            vmem((2, 3, LANES), f32),
            vmem((2, 3, LANES), f32),
            vmem((2, 16, LANES), f32),
            vmem((2, 3, 16, LANES), f32),
            vmem((2, 1, LANES), f32),
            vmem((2, 1, LANES), f32),
            vmem((2, 2, 1, LANES), f32),
            vmem((32, LANES), jnp.int32),
            vmem((32, LANES), f32),
            vmem((16, LANES), jnp.int32),
            vmem((16, LANES), f32),
            vmem((48, 32 * LANES), bf16),
            vmem((LANES, 32 * LANES), bf16),
            vmem((16, 16 * LANES), bf16),
            vmem((LANES, 16 * LANES), bf16),
            vmem((48, 16 * LANES), bf16),
            vmem((LANES, 16 * LANES), bf16),
            vmem((16, 16 * LANES), bf16),
            vmem((LANES, 16 * LANES), bf16),
            vmem((2, 48, 16 * LANES), bf16),
            vmem((2, LANES, 16 * LANES), bf16),
        ],
        compiler_params=pltpu.CompilerParams(collective_id=0, has_side_effects=True),
        name="newmark_step",
    )(*operands)
    outs = pl.pallas_call(
        write_kernel,
        out_shape=tuple(jax.ShapeDtypeStruct(shape, f32) for shape in shapes),
        in_specs=[pl.BlockSpec(memory_space=vmem)] * 4,
        out_specs=[pl.BlockSpec(memory_space=pl.ANY)] * 4,
        scratch_shapes=[pltpu.SemaphoreType.DMA((4,))],
        name="write_results",
    )(*[pltpu.with_memory_space_constraint(x, vmem) for x in outs])
    return outs[0], outs[1], outs[2].reshape(512), outs[3].reshape(512)


def solution(mesh):
    cut = ("region", "dom")
    line, plane = P(cut), P(None, cut)
    in_specs = (
        (plane,) * 3
        + (line,)
        + (plane,) * 3
        + (line,) * 5
        + (plane,) * 2
        + (line,)
        + (plane,) * 4
        + (P(None, None, cut),)
    )
    n_region, n_dom = mesh.shape["region"], mesh.shape["dom"]
    return jax.shard_map(
        lambda *args: on_device(n_region, n_dom, *args),
        mesh=mesh,
        in_specs=in_specs,
        out_specs=(plane, plane, line, line),
        check_vma=False,
    )
```

```python
import math

import jax
import jax.numpy as jnp
import numpy as np
from jax import lax
from jax.experimental import pallas as pl
from jax.experimental.pallas import tpu as pltpu
from jax.sharding import PartitionSpec as P

time_step = 0.4
MESH = pl.DeviceIdType.MESH
LANES = 128
f32 = jnp.float32
bf16 = jnp.bfloat16


def gll_tables():
    points = np.array([-1.0, -math.sqrt(3.0 / 7.0), 0.0, math.sqrt(3.0 / 7.0), 1.0])
    weights = np.array([0.1, 49.0 / 90.0, 32.0 / 45.0, 49.0 / 90.0, 0.1])
    products = np.array(
        [np.prod([points[i] - points[j] for j in range(5) if j != i]) for i in range(5)]
    )
    derivative = np.zeros((5, 5))
    for i in range(5):
        for j in range(5):
            if i != j:
                derivative[i, j] = products[i] / (products[j] * (points[i] - points[j]))
            else:
                derivative[i, j] = sum(1.0 / (points[i] - points[k]) for k in range(5) if k != i)
    weight_cube = weights[:, None, None] * weights[None, :, None] * weights[None, None, :]
    return derivative.astype(np.float32), weight_cube.astype(np.float32)


def derivative_matrices():
    derivative, weight_cube = gll_tables()
    eye = np.eye(5, dtype=np.float32)
    whole = np.zeros((3, LANES, LANES), np.float32)
    whole[0, :125, :125] = np.kron(derivative, np.kron(eye, eye))
    whole[1, :125, :125] = np.kron(eye, np.kron(derivative, eye))
    whole[2, :125, :125] = np.kron(eye, np.kron(eye, derivative))
    whole = whole.reshape(3 * LANES, LANES)
    high = whole.astype(jnp.bfloat16)
    low = (whole - high.astype(np.float32)).astype(jnp.bfloat16)
    weights = np.zeros((8, LANES), np.float32)
    weights[:, :125] = weight_cube.reshape(1, 125)
    return high, low, weights


def when(condition, action):
    if condition is None:
        action()
    else:
        pl.when(condition)(action)


def split(x):
    high = x.astype(bf16)
    return high, (x - high.astype(f32)).astype(bf16)


def dot(a, b, dims):
    return lax.dot_general(a, b, (dims, ((), ())), preferred_element_type=f32)


def dot_split(x, high, low, dims):
    x_high, x_low = split(x)
    return dot(x_high, high, dims) + dot(x_low, high, dims) + dot(x_high, low, dims)


def lookup(tables, hi, lo):
    out = [jnp.zeros(hi.shape, f32) for _ in tables]
    for h in range(len(tables[0])):
        here = hi == h
        for c, rows in enumerate(tables):
            picked = jnp.take_along_axis(
                jnp.broadcast_to(rows[h], hi.shape), lo, axis=1, mode="promise_in_bounds"
            )
            out[c] = jnp.where(here, picked, out[c])
    return out


def mark_low(marks_ref, lo):
    sublane = lax.broadcasted_iota(jnp.int32, (LANES, LANES), 0)
    for row in range(lo.shape[0]):
        line = jnp.broadcast_to(lo[row : row + 1], (LANES, LANES))
        marks_ref[:, row * LANES : (row + 1) * LANES] = jnp.where(line == sublane, 1.0, 0.0).astype(
            bf16
        )


def spread_high(terms_ref, hi, values):
    sublane = lax.broadcasted_iota(jnp.int32, (8, LANES), 0)
    parts = []
    for value in values:
        high = value.astype(bf16).astype(f32)
        parts.append((high, value - high))
    for row in range(hi.shape[0]):
        here = jnp.broadcast_to(hi[row : row + 1], (8, LANES)) == sublane
        for c, pair in enumerate(parts):
            both = [
                jnp.where(here, jnp.broadcast_to(part[row : row + 1], (8, LANES)), 0.0)
                for part in pair
            ]
            terms_ref[16 * c : 16 * c + 16, row * LANES : (row + 1) * LANES] = jnp.concatenate(
                both, axis=0
            ).astype(bf16)


def halved(terms_ref, marks_ref):
    middle = terms_ref.shape[1] // 2
    return sum(
        dot(terms_ref[:, half], marks_ref[:, half], ((1,), (1,)))
        for half in (slice(0, middle), slice(middle, 2 * middle))
    )


def collect(terms_ref, marks_ref):
    sums = halved(terms_ref, marks_ref)
    return [
        sums[16 * c : 16 * c + 8] + sums[16 * c + 8 : 16 * c + 16]
        for c in range(terms_ref.shape[0] // 16)
    ]


def spread_rows(terms_ref, values):
    sublane = lax.broadcasted_iota(jnp.int32, (8, LANES), 0)
    for c, value in enumerate(values):
        high = value.astype(bf16).astype(f32)
        pair = (high, value - high)
        for row in range(value.shape[0]):
            first = row // 8 * 8
            both = [
                jnp.where(sublane == row % 8, part[first : first + 8], 0.0) for part in pair
            ]
            terms_ref[16 * c : 16 * c + 16, row * LANES : (row + 1) * LANES] = jnp.concatenate(
                both, axis=0
            ).astype(bf16)


def rows_of(ref, lead):
    line = ref[lead]
    return jnp.concatenate([line[:, LANES * t : LANES * (t + 1)] for t in range(8)], axis=0)


def both_sides(ref, *lead):
    return jnp.concatenate(
        [rows_of(ref, (*lead, slice(p, p + 1), slice(None))) for p in range(2)], axis=0
    )


def step_kernel(n_region, n_dom, n_inputs, *refs):
    sources = refs[:n_inputs]
    velocity_out, acceleration_out, dot_out, ddot_out = refs[n_inputs : n_inputs + 4]
    held = refs[n_inputs + 4 : 2 * n_inputs + 4]
    (
        load_sem,
        passed_sem,
        known_sem,
        send_sem,
        recv_sem,
        motion_send,
        motion_recv,
        static_send,
        static_recv,
        normals_send,
        normals_recv,
        rims_send,
        rims_recv,
        block_send,
        block_recv,
        fluid_send,
        fluid_recv,
        far_recv,
        index_pad,
        field_pad,
        fluid_index_pad,
        fluid_field_pad,
        element_terms,
        element_marks,
        fluid_terms,
        fluid_marks,
        slot_terms,
        slot_marks,
        arrived_terms,
        arrived_marks,
        near_terms,
        near_marks,
    ) = refs[2 * n_inputs + 4 :]
    (
        displacement,
        velocity,
        acceleration,
        solid_interface,
        interface_normal,
        potential,
        potential_dot,
        potential_ddot,
        fluid_connectivity,
        density_inverse,
        fluid_inverse_size,
        matrix_high,
        matrix_low,
        weight_cube,
        fluid_interface,
        fluid_halo,
        fluid_mass_inverse,
        connectivity,
        lame_lambda,
        shear_modulus,
        inverse_size,
        solid_halo,
        solid_mass_inverse,
    ) = held

    region, dom = lax.axis_index("region"), lax.axis_index("dom")
    has_above, has_below = region < n_region - 1, region > 0
    to_region = {1: (has_above, has_below), -1: (has_below, has_above), 0: (None, None)}
    device = {
        (up, along): (
            region + up,
            lax.rem(dom + n_dom + along, n_dom),
        )
        for up in (-1, 0, 1)
        for along in (-2, -1, 0, 1, 2)
    }
    for ref in (motion_recv, static_recv, block_recv, far_recv):
        ref[...] = jnp.zeros(ref.shape, f32)
    barrier = pltpu.get_barrier_semaphore()
    for (up, along), other in device.items():
        if abs(up) + abs(along) == 1:
            when(
                to_region[up][0],
                lambda other=other: pl.semaphore_signal(
                    barrier, inc=1, device_id=other, device_id_type=MESH
                ),
            )
    loads = [
        pltpu.make_async_copy(source, target, load_sem.at[i])
        for i, (source, target) in enumerate(zip(sources, held))
    ]
    for load in loads:
        load.start()

    started = []

    def send(*messages):
        copies = []
        for source, target, up, along in messages:
            number = len(started)
            copy = pltpu.make_async_remote_copy(
                src_ref=source,
                dst_ref=target,
                send_sem=send_sem.at[number],
                recv_sem=recv_sem.at[number],
                device_id=device[up, along],
                device_id_type=MESH,
            )
            when(to_region[up][0], copy.start)
            started.append((copy, to_region[up][0]))
            copies.append((copy, to_region[up][1]))
        return copies

    def receive(copies):
        for copy, condition in copies:
            when(condition, copy.wait_recv)

    for i in range(5):
        loads[i].wait()
    half_square = 0.5 * time_step * time_step
    predicted = displacement[...] + time_step * velocity[...] + half_square * acceleration[...]
    solid_tables = [
        [predicted[c : c + 1, LANES * h : LANES * (h + 1)] for h in range(8)] for c in range(3)
    ]
    slots = both_sides(solid_interface)
    slot_hi, slot_lo = slots >> 7, slots & 127
    normals = [both_sides(interface_normal, c) for c in range(3)]
    moved = lookup(solid_tables, slot_hi, slot_lo)
    motion = normals[0] * moved[0] + normals[1] * moved[1] + normals[2] * moved[2]
    motion_send[0] = motion[8:]
    motion_send[1] = motion[:8]

    peers = 2 + lax.div(region + n_region - 1, n_region)
    peers = peers + lax.div(2 * n_region - 2 - region, n_region)
    pl.semaphore_wait(barrier, peers)

    def greet(semaphore):
        for along in (-1, 1):
            pl.semaphore_signal(
                semaphore, inc=1, device_id=device[0, along], device_id_type=MESH
            )

    greet(passed_sem)
    motion_copies = send(
        (motion_send.at[0], motion_recv.at[0], 1, 0),
        (motion_send.at[1], motion_recv.at[1], -1, 0),
    )

    for i in range(5, 14):
        loads[i].wait()
    fluid_predicted = (
        potential[...] + time_step * potential_dot[...] + half_square * potential_ddot[...]
    )
    fluid_table = [[fluid_predicted[h : h + 1] for h in range(4)]]
    fluid_index_pad[...] = jnp.full(fluid_index_pad.shape, -1, jnp.int32)
    fluid_index_pad[:, :125] = fluid_connectivity[...]
    fluid_field_pad[...] = jnp.zeros(fluid_field_pad.shape, f32)
    fluid_field_pad[:, :125] = density_inverse[...].astype(f32)
    fluid_index = fluid_index_pad[...]
    fluid_hi, fluid_lo = fluid_index >> 7, fluid_index & 127
    local = lookup(fluid_table, fluid_hi, fluid_lo)[0]
    high, low = matrix_high[...], matrix_low[...]
    gradient = dot_split(local, high, low, ((1,), (1,)))

    def column(line, count):
        rows = lax.broadcasted_iota(jnp.int32, (count, count), 0)
        columns = lax.broadcasted_iota(jnp.int32, (count, count), 1)
        wide = jnp.broadcast_to(line, (count, count))
        return jnp.sum(jnp.where(rows == columns, wide, 0.0), axis=1, keepdims=True)

    weights = weight_cube[0:1]
    fluid_factor = weights * fluid_field_pad[...] * (-1.0 / column(fluid_inverse_size[...], 16))
    weighted = jnp.concatenate(
        [gradient[:, LANES * b : LANES * (b + 1)] * fluid_factor for b in range(3)], axis=1
    )
    element = dot_split(weighted, high, low, ((1,), (0,)))
    mark_low(fluid_marks, fluid_lo)
    spread_high(fluid_terms, fluid_hi, [element])
    fluid_force = collect(fluid_terms, fluid_marks)[0]

    def rim_index(halo_ref, pad_ref, count):
        pad_ref[...] = jnp.full(pad_ref.shape, -1, jnp.int32)
        pad_ref[0:2, :count] = halo_ref[...]
        return pad_ref[...]

    def slot_of_node(rim):
        out = []
        marks_lane = lax.broadcasted_iota(jnp.int32, (LANES, LANES), 0)
        sublane = lax.broadcasted_iota(jnp.int32, (8, LANES), 0)
        number = lax.broadcasted_iota(jnp.int32, (8, LANES), 1).astype(f32) + 1.0
        for side in range(2):
            line = rim[side : side + 1]
            marks = jnp.where(
                jnp.broadcast_to(line & 127, (LANES, LANES)) == marks_lane, 1.0, 0.0
            ).astype(bf16)
            terms = jnp.where(jnp.broadcast_to(line >> 7, (8, LANES)) == sublane, number, 0.0)
            out.append(dot(terms.astype(bf16), marks, ((1,), (1,))))
        return out

    def pick(line, place):
        index = jnp.maximum(place.astype(jnp.int32) - 1, 0)
        wide = jnp.broadcast_to(line, place.shape)
        picked = jnp.take_along_axis(wide, index, axis=1, mode="promise_in_bounds")
        return jnp.where(place > 0.5, picked, 0.0)

    for i in range(14, 17):
        loads[i].wait()
    fluid_slots = both_sides(fluid_interface)
    arrived_hi, arrived_lo = fluid_slots >> 7, fluid_slots & 127
    fluid_rim = rim_index(fluid_halo, index_pad.at[0:8], 48)
    fluid_places = slot_of_node(fluid_rim)
    slot_mass = lookup(
        [[fluid_mass_inverse[h : h + 1] for h in range(4)]]
        + [[place[h : h + 1] for h in range(4)] for place in fluid_places],
        arrived_hi,
        arrived_lo,
    )
    for i in range(3):
        static_send[0, 8 * i : 8 * i + 8] = slot_mass[i][8:]
        static_send[1, 8 * i : 8 * i + 8] = slot_mass[i][:8]
    loads[21].wait()
    solid_rim = rim_index(solid_halo, index_pad.at[0:8], 96)
    solid_places = slot_of_node(solid_rim)
    slot_places = lookup(
        [[place[h : h + 1] for h in range(8)] for place in solid_places], slot_hi, slot_lo
    )
    for side in range(2):
        for c in range(3):
            normals_send[side, 16 * c : 16 * c + 16] = -normals[c]
        normals_send[side, 48:] = slot_places[1 - side]

    pl.semaphore_wait(passed_sem, 2)
    greet(known_sem)
    normals_copies = send(
        *((normals_send.at[i], normals_recv.at[i], 0, 1 - 2 * i) for i in range(2))
    )
    static_copies = send(
        *(
            (static_send.at[i], static_recv.at[i, 1 + along], 1 - 2 * i, along)
            for along in (-1, 0, 1)
            for i in range(2)
        )
    )

    for i in (17, 18, 19, 20, 22):
        loads[i].wait()
    index_pad[...] = jnp.full(index_pad.shape, -1, jnp.int32)
    index_pad[:, :125] = connectivity[...]
    index = index_pad[...]
    hi, lo = index >> 7, index & 127
    values = lookup(solid_tables, hi, lo)
    gradient = dot_split(jnp.concatenate(values, axis=0), high, low, ((1,), (1,)))
    field_pad[...] = jnp.zeros(field_pad.shape, f32)
    field_pad[:, :125] = lame_lambda[...].astype(f32)
    lame = field_pad[...]
    field_pad[:, :125] = shear_modulus[...].astype(f32)
    shear = field_pad[...]
    factor = weights * (-1.0 / column(inverse_size[...], 32))
    lame, shear = lame * factor, shear * factor
    grad = [
        [gradient[32 * c : 32 * c + 32, LANES * b : LANES * (b + 1)] for b in range(3)]
        for c in range(3)
    ]
    trace = lame * (grad[0][0] + grad[1][1] + grad[2][2])
    stress = [[None] * 3 for _ in range(3)]
    for a in range(3):
        stress[a][a] = trace + shear * (grad[a][a] + grad[a][a])
        for b in range(a):
            stress[a][b] = stress[b][a] = shear * (grad[a][b] + grad[b][a])
    weighted = jnp.concatenate([jnp.concatenate(row, axis=1) for row in stress], axis=0)
    element = dot_split(weighted, high, low, ((1,), (0,)))
    mark_low(element_marks, lo)
    spread_high(element_terms, hi, [element[32 * c : 32 * c + 32] for c in range(3)])

    force = collect(element_terms, element_marks)
    rim_values = lookup(
        [[t[h : h + 1] for h in range(8)] for t in force], solid_rim >> 7, solid_rim & 127
    )
    for c in range(3):
        rims_send[0, c : c + 1] = rim_values[c][1:2]
        rims_send[1, c : c + 1] = rim_values[c][0:1]
    rims_copies = send(*((rims_send.at[i], rims_recv.at[i], 0, 1 - 2 * i) for i in range(2)))
    mark_low(arrived_marks, arrived_lo)

    pl.semaphore_wait(known_sem, 2)
    receive(motion_copies)
    spread_high(
        arrived_terms, arrived_hi, [jnp.concatenate([motion_recv[0], motion_recv[1]], axis=0)]
    )
    fluid_total = fluid_force + collect(arrived_terms, arrived_marks)[0]
    total_rows = [[fluid_total[h : h + 1] for h in range(4)]]
    at_slots = lookup(total_rows, arrived_hi, arrived_lo)[0]
    rim_values = lookup(total_rows, fluid_rim >> 7, fluid_rim & 127)[0]
    for i in range(2):
        block_send[i, :8] = at_slots[8 - 8 * i : 16 - 8 * i]
        block_send[i, 8:9] = rim_values[1:2]
        block_send[i, 9:10] = rim_values[0:1]
        fluid_send[i] = rim_values[1 - i : 2 - i]
    block_copies = send(
        *(
            (fluid_send.at[j], far_recv.at[i, j], 1 - 2 * i, 2 - 4 * j)
            for j in range(2)
            for i in range(2)
        ),
        *(
            (block_send.at[i], block_recv.at[i, 1 + along], 1 - 2 * i, along)
            for along in (-1, 1, 0)
            for i in range(2)
        ),
    )
    fluid_copies = send(*((fluid_send.at[i], fluid_recv.at[i], 0, 1 - 2 * i) for i in range(2)))

    mark_low(slot_marks, slot_lo)
    receive(normals_copies)
    for i in range(2):
        mark_low(near_marks.at[i], normals_recv[i, 48:].astype(jnp.int32) - 1)
    mass = solid_mass_inverse[...]
    base = [
        rows_of(velocity, (slice(c, c + 1), slice(None)))
        + 0.5 * time_step * rows_of(acceleration, (slice(c, c + 1), slice(None)))
        for c in range(3)
    ]
    receive(fluid_copies)
    assembled = fluid_total
    for i in range(2):
        assembled = assembled + pick(fluid_recv[i], fluid_places[i])
    ddot = fluid_mass_inverse[...] * assembled[:4]
    ddot_out[...] = ddot
    dot_out[...] = potential_dot[...] + 0.5 * time_step * (potential_ddot[...] + ddot)
    receive(static_copies)
    receive(rims_copies)

    receive(block_copies)

    def pressure_of(column):
        sides = []
        for i in range(2):
            block = block_recv.at[i, 1 - column]
            if column == -1:
                low_rim = far_recv[i, 0]
            else:
                low_rim = block_recv[i, 2 - column, 8:9]
            if column == 1:
                high_rim = far_recv[i, 1]
            else:
                high_rim = block_recv[i, -column, 9:10]
            slot_mass, low_place, high_place = (
                static_recv[i, 1 - column, 8 * j : 8 * j + 8] for j in range(3)
            )
            value = block[:8] + pick(low_rim, low_place)
            sides.append(slot_mass * (value + pick(high_rim, high_place)))
        return jnp.concatenate(sides, axis=0)

    arrived = pressure_of(0)
    spread_high(slot_terms, slot_hi, [-(normal * arrived) for normal in normals])
    for i in range(2):
        arrived = pressure_of(2 * i - 1)
        spread_rows(
            near_terms.at[i],
            [normals_recv[i, 16 * c : 16 * c + 16] * arrived for c in range(3)],
        )
    coupling = collect(slot_terms, slot_marks)
    near = []
    for i in range(2):
        sums = dot(near_terms[i], near_marks[i], ((1,), (1,)))
        near.append(
            [jnp.sum(sums[16 * c : 16 * c + 16], axis=0, keepdims=True) for c in range(3)]
        )
    for c in range(3):
        assembled = force[c] + coupling[c]
        for i in range(2):
            line = rims_recv[i, c : c + 1] + near[i][c]
            assembled = assembled + pick(line, solid_places[i])
        new = mass * assembled
        speed = base[c] + 0.5 * time_step * new
        for h in range(8):
            acceleration_out[c : c + 1, LANES * h : LANES * (h + 1)] = new[h : h + 1]
            velocity_out[c : c + 1, LANES * h : LANES * (h + 1)] = speed[h : h + 1]
    for copy, condition in started:
        when(condition, copy.wait_send)


def write_kernel(*refs):
    sem = refs[-1]
    copies = [
        pltpu.make_async_copy(refs[i], refs[4 + i], sem.at[i]) for i in range(4)
    ]
    for copy in copies:
        copy.start()
    for copy in copies:
        copy.wait()


def on_device(
    n_region,
    n_dom,
    displacement,
    velocity,
    acceleration,
    solid_mass_inverse,
    connectivity,
    lame_lambda,
    shear_modulus,
    inverse_size,
    potential,
    potential_dot,
    potential_ddot,
    fluid_mass_inverse,
    fluid_connectivity,
    density_inverse,
    fluid_inverse_size,
    solid_halo,
    fluid_halo,
    solid_interface,
    fluid_interface,
    interface_normal,
):
    high, low, weights = derivative_matrices()
    operands = (
        displacement,
        velocity,
        acceleration,
        solid_interface,
        interface_normal,
        potential.reshape(4, LANES),
        potential_dot.reshape(4, LANES),
        potential_ddot.reshape(4, LANES),
        fluid_connectivity.T,
        density_inverse.T,
        fluid_inverse_size.reshape(1, 16),
        jnp.asarray(high),
        jnp.asarray(low),
        jnp.asarray(weights),
        fluid_interface,
        fluid_halo,
        fluid_mass_inverse.reshape(4, LANES),
        connectivity.T,
        lame_lambda.T,
        shear_modulus.T,
        inverse_size.reshape(1, 32),
        solid_halo,
        solid_mass_inverse.reshape(8, LANES),
    )
    count = len(operands)
    vmem = pltpu.VMEM
    shapes = ((3, 1024), (3, 1024), (4, LANES), (4, LANES))
    outs = pl.pallas_call(
        lambda *refs: step_kernel(n_region, n_dom, count, *refs),
        out_shape=tuple(pltpu.VMEM(shape, f32) for shape in shapes),
        in_specs=[pl.BlockSpec(memory_space=pl.ANY)] * count,
        out_specs=[pl.BlockSpec(memory_space=vmem)] * 4,
        scratch_shapes=[vmem(x.shape, x.dtype) for x in operands]
        + [
            pltpu.SemaphoreType.DMA((count,)),
            pltpu.SemaphoreType.REGULAR,
            pltpu.SemaphoreType.REGULAR,
            pltpu.SemaphoreType.DMA((24,)),
            pltpu.SemaphoreType.DMA((24,)),
            vmem((2, 8, LANES), f32),
            vmem((2, 8, LANES), f32),
            vmem((2, 24, LANES), f32),
            vmem((2, 3, 24, LANES), f32),
            vmem((2, 64, LANES), f32),
            vmem((2, 64, LANES), f32),
            vmem((2, 3, LANES), f32),
            vmem((2, 3, LANES), f32),
            vmem((2, 16, LANES), f32),
            vmem((2, 3, 16, LANES), f32),
            vmem((2, 1, LANES), f32),
            vmem((2, 1, LANES), f32),
            vmem((2, 2, 1, LANES), f32),
            vmem((32, LANES), jnp.int32),
            vmem((32, LANES), f32),
            vmem((16, LANES), jnp.int32),
            vmem((16, LANES), f32),
            vmem((48, 32 * LANES), bf16),
            vmem((LANES, 32 * LANES), bf16),
            vmem((16, 16 * LANES), bf16),
            vmem((LANES, 16 * LANES), bf16),
            vmem((48, 16 * LANES), bf16),
            vmem((LANES, 16 * LANES), bf16),
            vmem((16, 16 * LANES), bf16),
            vmem((LANES, 16 * LANES), bf16),
            vmem((2, 48, 16 * LANES), bf16),
            vmem((2, LANES, 16 * LANES), bf16),
        ],
        compiler_params=pltpu.CompilerParams(collective_id=0, has_side_effects=True),
        name="newmark_step",
    )(*operands)
    outs = pl.pallas_call(
        write_kernel,
        out_shape=tuple(jax.ShapeDtypeStruct(shape, f32) for shape in shapes),
        in_specs=[pl.BlockSpec(memory_space=vmem)] * 4,
        out_specs=[pl.BlockSpec(memory_space=pl.ANY)] * 4,
        scratch_shapes=[pltpu.SemaphoreType.DMA((4,))],
        name="write_results",
    )(*[pltpu.with_memory_space_constraint(x, vmem) for x in outs])
    return outs[0], outs[1], outs[2].reshape(512), outs[3].reshape(512)


def solution(mesh):
    cut = ("region", "dom")
    line, plane = P(cut), P(None, cut)
    in_specs = (
        (plane,) * 3
        + (line,)
        + (plane,) * 3
        + (line,) * 5
        + (plane,) * 2
        + (line,)
        + (plane,) * 4
        + (P(None, None, cut),)
    )
    n_region, n_dom = mesh.shape["region"], mesh.shape["dom"]
    return jax.shard_map(
        lambda *args: on_device(n_region, n_dom, *args),
        mesh=mesh,
        in_specs=in_specs,
        out_specs=(plane, plane, line, line),
        check_vma=False,
    )
```

```python
import math

import jax
import jax.numpy as jnp
import numpy as np
from jax import lax
from jax.experimental import pallas as pl
from jax.experimental.pallas import tpu as pltpu
from jax.sharding import PartitionSpec as P

time_step = 0.4
MESH = pl.DeviceIdType.MESH
LANES = 128
f32 = jnp.float32
bf16 = jnp.bfloat16


def gll_tables():
    points = np.array([-1.0, -math.sqrt(3.0 / 7.0), 0.0, math.sqrt(3.0 / 7.0), 1.0])
    weights = np.array([0.1, 49.0 / 90.0, 32.0 / 45.0, 49.0 / 90.0, 0.1])
    products = np.array(
        [np.prod([points[i] - points[j] for j in range(5) if j != i]) for i in range(5)]
    )
    derivative = np.zeros((5, 5))
    for i in range(5):
        for j in range(5):
            if i != j:
                derivative[i, j] = products[i] / (products[j] * (points[i] - points[j]))
            else:
                derivative[i, j] = sum(1.0 / (points[i] - points[k]) for k in range(5) if k != i)
    weight_cube = weights[:, None, None] * weights[None, :, None] * weights[None, None, :]
    return derivative.astype(np.float32), weight_cube.astype(np.float32)


def derivative_matrices():
    derivative, weight_cube = gll_tables()
    eye = np.eye(5, dtype=np.float32)
    whole = np.zeros((3, LANES, LANES), np.float32)
    whole[0, :125, :125] = np.kron(derivative, np.kron(eye, eye))
    whole[1, :125, :125] = np.kron(eye, np.kron(derivative, eye))
    whole[2, :125, :125] = np.kron(eye, np.kron(eye, derivative))
    whole = whole.reshape(3 * LANES, LANES)
    high = whole.astype(jnp.bfloat16)
    low = (whole - high.astype(np.float32)).astype(jnp.bfloat16)
    weights = np.zeros((8, LANES), np.float32)
    weights[:, :125] = weight_cube.reshape(1, 125)
    return high, low, weights


def when(condition, action):
    if condition is None:
        action()
    else:
        pl.when(condition)(action)


def split(x):
    high = x.astype(bf16)
    return high, (x - high.astype(f32)).astype(bf16)


def dot(a, b, dims):
    return lax.dot_general(a, b, (dims, ((), ())), preferred_element_type=f32)


def dot_split(x, high, low, dims):
    x_high, x_low = split(x)
    return dot(x_high, high, dims) + dot(x_low, high, dims) + dot(x_high, low, dims)


def lookup(tables, hi, lo):
    out = [jnp.zeros(hi.shape, f32) for _ in tables]
    for h in range(len(tables[0])):
        here = hi == h
        for c, rows in enumerate(tables):
            picked = jnp.take_along_axis(
                jnp.broadcast_to(rows[h], hi.shape), lo, axis=1, mode="promise_in_bounds"
            )
            out[c] = jnp.where(here, picked, out[c])
    return out


def mark_low(marks_ref, lo):
    sublane = lax.broadcasted_iota(jnp.int32, (LANES, LANES), 0)
    for row in range(lo.shape[0]):
        line = jnp.broadcast_to(lo[row : row + 1], (LANES, LANES))
        marks_ref[:, row * LANES : (row + 1) * LANES] = jnp.where(line == sublane, 1.0, 0.0).astype(
            bf16
        )


def spread_high(terms_ref, hi, values):
    sublane = lax.broadcasted_iota(jnp.int32, (8, LANES), 0)
    parts = []
    for value in values:
        high = value.astype(bf16).astype(f32)
        parts.append((high, value - high))
    for row in range(hi.shape[0]):
        here = jnp.broadcast_to(hi[row : row + 1], (8, LANES)) == sublane
        for c, pair in enumerate(parts):
            both = [
                jnp.where(here, jnp.broadcast_to(part[row : row + 1], (8, LANES)), 0.0)
                for part in pair
            ]
            terms_ref[16 * c : 16 * c + 16, row * LANES : (row + 1) * LANES] = jnp.concatenate(
                both, axis=0
            ).astype(bf16)


def halved(terms_ref, marks_ref):
    middle = terms_ref.shape[1] // 2
    return sum(
        dot(terms_ref[:, half], marks_ref[:, half], ((1,), (1,)))
        for half in (slice(0, middle), slice(middle, 2 * middle))
    )


def collect(terms_ref, marks_ref):
    sums = halved(terms_ref, marks_ref)
    return [
        sums[16 * c : 16 * c + 8] + sums[16 * c + 8 : 16 * c + 16]
        for c in range(terms_ref.shape[0] // 16)
    ]


def spread_rows(terms_ref, values):
    sublane = lax.broadcasted_iota(jnp.int32, (8, LANES), 0)
    for c, value in enumerate(values):
        high = value.astype(bf16).astype(f32)
        pair = (high, value - high)
        for row in range(value.shape[0]):
            first = row // 8 * 8
            both = [
                jnp.where(sublane == row % 8, part[first : first + 8], 0.0) for part in pair
            ]
            terms_ref[16 * c : 16 * c + 16, row * LANES : (row + 1) * LANES] = jnp.concatenate(
                both, axis=0
            ).astype(bf16)


def rows_of(ref, lead):
    line = ref[lead]
    return jnp.concatenate([line[:, LANES * t : LANES * (t + 1)] for t in range(8)], axis=0)


def both_sides(ref, *lead):
    return jnp.concatenate(
        [rows_of(ref, (*lead, slice(p, p + 1), slice(None))) for p in range(2)], axis=0
    )


def step_kernel(n_region, n_dom, n_inputs, local, *refs):
    load_sem, send_sem = local
    sources = refs[:n_inputs]
    velocity_out, acceleration_out, dot_out, ddot_out = refs[n_inputs : n_inputs + 4]
    held = refs[n_inputs + 4 : 2 * n_inputs + 4]
    (
        passed_sem,
        known_sem,
        recv_sem,
        motion_send,
        motion_recv,
        static_send,
        static_recv,
        normals_send,
        normals_recv,
        rims_send,
        rims_recv,
        block_send,
        block_recv,
        fluid_send,
        fluid_recv,
        far_recv,
        index_pad,
        field_pad,
        fluid_index_pad,
        fluid_field_pad,
        element_terms,
        element_marks,
        fluid_terms,
        fluid_marks,
        slot_terms,
        slot_marks,
        arrived_terms,
        arrived_marks,
        near_terms,
        near_marks,
    ) = refs[2 * n_inputs + 4 :]
    (
        displacement,
        velocity,
        acceleration,
        solid_interface,
        interface_normal,
        potential,
        potential_dot,
        potential_ddot,
        fluid_connectivity,
        density_inverse,
        fluid_inverse_size,
        matrix_high,
        matrix_low,
        weight_cube,
        fluid_interface,
        fluid_halo,
        fluid_mass_inverse,
        connectivity,
        lame_lambda,
        shear_modulus,
        inverse_size,
        solid_halo,
        solid_mass_inverse,
    ) = held

    region, dom = lax.axis_index("region"), lax.axis_index("dom")
    has_above, has_below = region < n_region - 1, region > 0
    to_region = {1: (has_above, has_below), -1: (has_below, has_above), 0: (None, None)}
    device = {
        (up, along): (
            region + up,
            lax.rem(dom + n_dom + along, n_dom),
        )
        for up in (-1, 0, 1)
        for along in (-2, -1, 0, 1, 2)
    }
    for ref in (motion_recv, static_recv, block_recv, far_recv):
        ref[...] = jnp.zeros(ref.shape, f32)
    barrier = pltpu.get_barrier_semaphore()
    for (up, along), other in device.items():
        if abs(up) + abs(along) == 1:
            when(
                to_region[up][0],
                lambda other=other: pl.semaphore_signal(
                    barrier, inc=1, device_id=other, device_id_type=MESH
                ),
            )
    loads = [
        pltpu.make_async_copy(source, target, load_sem.at[i])
        for i, (source, target) in enumerate(zip(sources, held))
    ]
    for load in loads:
        load.start()

    started = []

    def send(*messages):
        copies = []
        for source, target, up, along in messages:
            number = len(started)
            copy = pltpu.make_async_remote_copy(
                src_ref=source,
                dst_ref=target,
                send_sem=send_sem.at[number],
                recv_sem=recv_sem.at[number],
                device_id=device[up, along],
                device_id_type=MESH,
            )
            when(to_region[up][0], copy.start)
            started.append((copy, to_region[up][0]))
            copies.append((copy, to_region[up][1]))
        return copies

    def receive(copies):
        for copy, condition in copies:
            when(condition, copy.wait_recv)

    for i in range(5):
        loads[i].wait()
    half_square = 0.5 * time_step * time_step
    predicted = displacement[...] + time_step * velocity[...] + half_square * acceleration[...]
    solid_tables = [
        [predicted[c : c + 1, LANES * h : LANES * (h + 1)] for h in range(8)] for c in range(3)
    ]
    slots = both_sides(solid_interface)
    slot_hi, slot_lo = slots >> 7, slots & 127
    normals = [both_sides(interface_normal, c) for c in range(3)]
    moved = lookup(solid_tables, slot_hi, slot_lo)
    motion = normals[0] * moved[0] + normals[1] * moved[1] + normals[2] * moved[2]
    motion_send[0] = motion[8:]
    motion_send[1] = motion[:8]

    peers = 2 + lax.div(region + n_region - 1, n_region)
    peers = peers + lax.div(2 * n_region - 2 - region, n_region)
    pl.semaphore_wait(barrier, peers)

    def greet(semaphore):
        for along in (-1, 1):
            pl.semaphore_signal(
                semaphore, inc=1, device_id=device[0, along], device_id_type=MESH
            )

    greet(passed_sem)
    motion_copies = send(
        (motion_send.at[0], motion_recv.at[0], 1, 0),
        (motion_send.at[1], motion_recv.at[1], -1, 0),
    )

    for i in range(5, 14):
        loads[i].wait()
    fluid_predicted = (
        potential[...] + time_step * potential_dot[...] + half_square * potential_ddot[...]
    )
    fluid_table = [[fluid_predicted[h : h + 1] for h in range(4)]]
    fluid_index_pad[...] = jnp.full(fluid_index_pad.shape, -1, jnp.int32)
    fluid_index_pad[:, :125] = fluid_connectivity[...]
    fluid_field_pad[...] = jnp.zeros(fluid_field_pad.shape, f32)
    fluid_field_pad[:, :125] = density_inverse[...].astype(f32)
    fluid_index = fluid_index_pad[...]
    fluid_hi, fluid_lo = fluid_index >> 7, fluid_index & 127
    local = lookup(fluid_table, fluid_hi, fluid_lo)[0]
    high, low = matrix_high[...], matrix_low[...]
    gradient = dot_split(local, high, low, ((1,), (1,)))

    def column(line, count):
        rows = lax.broadcasted_iota(jnp.int32, (count, count), 0)
        columns = lax.broadcasted_iota(jnp.int32, (count, count), 1)
        wide = jnp.broadcast_to(line, (count, count))
        return jnp.sum(jnp.where(rows == columns, wide, 0.0), axis=1, keepdims=True)

    weights = weight_cube[0:1]
    fluid_factor = weights * fluid_field_pad[...] * (-1.0 / column(fluid_inverse_size[...], 16))
    weighted = jnp.concatenate(
        [gradient[:, LANES * b : LANES * (b + 1)] * fluid_factor for b in range(3)], axis=1
    )
    element = dot_split(weighted, high, low, ((1,), (0,)))
    mark_low(fluid_marks, fluid_lo)
    spread_high(fluid_terms, fluid_hi, [element])
    fluid_force = collect(fluid_terms, fluid_marks)[0]

    def rim_index(halo_ref, pad_ref, count):
        pad_ref[...] = jnp.full(pad_ref.shape, -1, jnp.int32)
        pad_ref[0:2, :count] = halo_ref[...]
        return pad_ref[...]

    def slot_of_node(rim):
        out = []
        marks_lane = lax.broadcasted_iota(jnp.int32, (LANES, LANES), 0)
        sublane = lax.broadcasted_iota(jnp.int32, (8, LANES), 0)
        number = lax.broadcasted_iota(jnp.int32, (8, LANES), 1).astype(f32) + 1.0
        for side in range(2):
            line = rim[side : side + 1]
            marks = jnp.where(
                jnp.broadcast_to(line & 127, (LANES, LANES)) == marks_lane, 1.0, 0.0
            ).astype(bf16)
            terms = jnp.where(jnp.broadcast_to(line >> 7, (8, LANES)) == sublane, number, 0.0)
            out.append(dot(terms.astype(bf16), marks, ((1,), (1,))))
        return out

    def pick(line, place):
        index = jnp.maximum(place.astype(jnp.int32) - 1, 0)
        wide = jnp.broadcast_to(line, place.shape)
        picked = jnp.take_along_axis(wide, index, axis=1, mode="promise_in_bounds")
        return jnp.where(place > 0.5, picked, 0.0)

    for i in range(14, 17):
        loads[i].wait()
    fluid_slots = both_sides(fluid_interface)
    arrived_hi, arrived_lo = fluid_slots >> 7, fluid_slots & 127
    fluid_rim = rim_index(fluid_halo, index_pad.at[0:8], 48)
    fluid_places = slot_of_node(fluid_rim)
    slot_mass = lookup(
        [[fluid_mass_inverse[h : h + 1] for h in range(4)]]
        + [[place[h : h + 1] for h in range(4)] for place in fluid_places],
        arrived_hi,
        arrived_lo,
    )
    for i in range(3):
        static_send[0, 8 * i : 8 * i + 8] = slot_mass[i][8:]
        static_send[1, 8 * i : 8 * i + 8] = slot_mass[i][:8]
    loads[21].wait()
    solid_rim = rim_index(solid_halo, index_pad.at[0:8], 96)
    solid_places = slot_of_node(solid_rim)
    slot_places = lookup(
        [[place[h : h + 1] for h in range(8)] for place in solid_places], slot_hi, slot_lo
    )
    for side in range(2):
        for c in range(3):
            normals_send[side, 16 * c : 16 * c + 16] = -normals[c]
        normals_send[side, 48:] = slot_places[1 - side]

    pl.semaphore_wait(passed_sem, 2)
    greet(known_sem)
    normals_copies = send(
        *((normals_send.at[i], normals_recv.at[i], 0, 1 - 2 * i) for i in range(2))
    )
    static_copies = send(
        *(
            (static_send.at[i], static_recv.at[i, 1 + along], 1 - 2 * i, along)
            for along in (-1, 0, 1)
            for i in range(2)
        )
    )

    for i in (17, 18, 19, 20, 22):
        loads[i].wait()
    index_pad[...] = jnp.full(index_pad.shape, -1, jnp.int32)
    index_pad[:, :125] = connectivity[...]
    index = index_pad[...]
    hi, lo = index >> 7, index & 127
    values = lookup(solid_tables, hi, lo)
    gradient = dot_split(jnp.concatenate(values, axis=0), high, low, ((1,), (1,)))
    field_pad[...] = jnp.zeros(field_pad.shape, f32)
    field_pad[:, :125] = lame_lambda[...].astype(f32)
    lame = field_pad[...]
    field_pad[:, :125] = shear_modulus[...].astype(f32)
    shear = field_pad[...]
    factor = weights * (-1.0 / column(inverse_size[...], 32))
    lame, shear = lame * factor, shear * factor
    grad = [
        [gradient[32 * c : 32 * c + 32, LANES * b : LANES * (b + 1)] for b in range(3)]
        for c in range(3)
    ]
    trace = lame * (grad[0][0] + grad[1][1] + grad[2][2])
    stress = [[None] * 3 for _ in range(3)]
    for a in range(3):
        stress[a][a] = trace + shear * (grad[a][a] + grad[a][a])
        for b in range(a):
            stress[a][b] = stress[b][a] = shear * (grad[a][b] + grad[b][a])
    weighted = jnp.concatenate([jnp.concatenate(row, axis=1) for row in stress], axis=0)
    element = dot_split(weighted, high, low, ((1,), (0,)))
    mark_low(element_marks, lo)
    spread_high(element_terms, hi, [element[32 * c : 32 * c + 32] for c in range(3)])

    force = collect(element_terms, element_marks)
    rim_values = lookup(
        [[t[h : h + 1] for h in range(8)] for t in force], solid_rim >> 7, solid_rim & 127
    )
    for c in range(3):
        rims_send[0, c : c + 1] = rim_values[c][1:2]
        rims_send[1, c : c + 1] = rim_values[c][0:1]
    rims_copies = send(*((rims_send.at[i], rims_recv.at[i], 0, 1 - 2 * i) for i in range(2)))
    mark_low(arrived_marks, arrived_lo)

    pl.semaphore_wait(known_sem, 2)
    receive(motion_copies)
    spread_high(
        arrived_terms, arrived_hi, [jnp.concatenate([motion_recv[0], motion_recv[1]], axis=0)]
    )
    fluid_total = fluid_force + collect(arrived_terms, arrived_marks)[0]
    total_rows = [[fluid_total[h : h + 1] for h in range(4)]]
    at_slots = lookup(total_rows, arrived_hi, arrived_lo)[0]
    rim_values = lookup(total_rows, fluid_rim >> 7, fluid_rim & 127)[0]
    for i in range(2):
        block_send[i, :8] = at_slots[8 - 8 * i : 16 - 8 * i]
        block_send[i, 8:9] = rim_values[1:2]
        block_send[i, 9:10] = rim_values[0:1]
        fluid_send[i] = rim_values[1 - i : 2 - i]
    block_copies = send(
        *(
            (fluid_send.at[j], far_recv.at[i, j], 1 - 2 * i, 2 - 4 * j)
            for j in range(2)
            for i in range(2)
        ),
        *(
            (block_send.at[i], block_recv.at[i, 1 + along], 1 - 2 * i, along)
            for along in (-1, 1, 0)
            for i in range(2)
        ),
    )
    fluid_copies = send(*((fluid_send.at[i], fluid_recv.at[i], 0, 1 - 2 * i) for i in range(2)))

    mark_low(slot_marks, slot_lo)
    receive(normals_copies)
    for i in range(2):
        mark_low(near_marks.at[i], normals_recv[i, 48:].astype(jnp.int32) - 1)
    mass = solid_mass_inverse[...]
    base = [
        rows_of(velocity, (slice(c, c + 1), slice(None)))
        + 0.5 * time_step * rows_of(acceleration, (slice(c, c + 1), slice(None)))
        for c in range(3)
    ]
    receive(fluid_copies)
    assembled = fluid_total
    for i in range(2):
        assembled = assembled + pick(fluid_recv[i], fluid_places[i])
    ddot = fluid_mass_inverse[...] * assembled[:4]
    ddot_out[...] = ddot
    dot_out[...] = potential_dot[...] + 0.5 * time_step * (potential_ddot[...] + ddot)
    receive(static_copies)
    receive(rims_copies)

    receive(block_copies)

    def pressure_of(column):
        sides = []
        for i in range(2):
            block = block_recv.at[i, 1 - column]
            if column == -1:
                low_rim = far_recv[i, 0]
            else:
                low_rim = block_recv[i, 2 - column, 8:9]
            if column == 1:
                high_rim = far_recv[i, 1]
            else:
                high_rim = block_recv[i, -column, 9:10]
            slot_mass, low_place, high_place = (
                static_recv[i, 1 - column, 8 * j : 8 * j + 8] for j in range(3)
            )
            value = block[:8] + pick(low_rim, low_place)
            sides.append(slot_mass * (value + pick(high_rim, high_place)))
        return jnp.concatenate(sides, axis=0)

    arrived = pressure_of(0)
    spread_high(slot_terms, slot_hi, [-(normal * arrived) for normal in normals])
    for i in range(2):
        arrived = pressure_of(2 * i - 1)
        spread_rows(
            near_terms.at[i],
            [normals_recv[i, 16 * c : 16 * c + 16] * arrived for c in range(3)],
        )
    coupling = collect(slot_terms, slot_marks)
    near = []
    for i in range(2):
        sums = dot(near_terms[i], near_marks[i], ((1,), (1,)))
        near.append(
            [jnp.sum(sums[16 * c : 16 * c + 16], axis=0, keepdims=True) for c in range(3)]
        )
    for c in range(3):
        assembled = force[c] + coupling[c]
        for i in range(2):
            line = rims_recv[i, c : c + 1] + near[i][c]
            assembled = assembled + pick(line, solid_places[i])
        new = mass * assembled
        speed = base[c] + 0.5 * time_step * new
        for h in range(8):
            acceleration_out[c : c + 1, LANES * h : LANES * (h + 1)] = new[h : h + 1]
            velocity_out[c : c + 1, LANES * h : LANES * (h + 1)] = speed[h : h + 1]
    for copy, condition in started:
        when(condition, copy.wait_send)


def write_kernel(*refs):
    sem = refs[-1]
    copies = [
        pltpu.make_async_copy(refs[i], refs[4 + i], sem.at[i]) for i in range(4)
    ]
    for copy in copies:
        copy.start()
    for copy in copies:
        copy.wait()


def on_device(
    n_region,
    n_dom,
    displacement,
    velocity,
    acceleration,
    solid_mass_inverse,
    connectivity,
    lame_lambda,
    shear_modulus,
    inverse_size,
    potential,
    potential_dot,
    potential_ddot,
    fluid_mass_inverse,
    fluid_connectivity,
    density_inverse,
    fluid_inverse_size,
    solid_halo,
    fluid_halo,
    solid_interface,
    fluid_interface,
    interface_normal,
):
    high, low, weights = derivative_matrices()
    operands = (
        displacement,
        velocity,
        acceleration,
        solid_interface,
        interface_normal,
        potential.reshape(4, LANES),
        potential_dot.reshape(4, LANES),
        potential_ddot.reshape(4, LANES),
        fluid_connectivity.T,
        density_inverse.T,
        fluid_inverse_size.reshape(1, 16),
        jnp.asarray(high),
        jnp.asarray(low),
        jnp.asarray(weights),
        fluid_interface,
        fluid_halo,
        fluid_mass_inverse.reshape(4, LANES),
        connectivity.T,
        lame_lambda.T,
        shear_modulus.T,
        inverse_size.reshape(1, 32),
        solid_halo,
        solid_mass_inverse.reshape(8, LANES),
    )
    count = len(operands)
    vmem = pltpu.VMEM
    shapes = ((3, 1024), (3, 1024), (4, LANES), (4, LANES))
    outs = pl.pallas_call(
        lambda *refs: pl.run_scoped(
            lambda *local: step_kernel(n_region, n_dom, count, local, *refs),
            pltpu.SemaphoreType.DMA((count,)),
            pltpu.SemaphoreType.DMA((24,)),
        ),
        out_shape=tuple(pltpu.VMEM(shape, f32) for shape in shapes),
        in_specs=[pl.BlockSpec(memory_space=pl.ANY)] * count,
        out_specs=[pl.BlockSpec(memory_space=vmem)] * 4,
        scratch_shapes=[vmem(x.shape, x.dtype) for x in operands]
        + [
            pltpu.SemaphoreType.REGULAR,
            pltpu.SemaphoreType.REGULAR,
            pltpu.SemaphoreType.DMA((24,)),
            vmem((2, 8, LANES), f32),
            vmem((2, 8, LANES), f32),
            vmem((2, 24, LANES), f32),
            vmem((2, 3, 24, LANES), f32),
            vmem((2, 64, LANES), f32),
            vmem((2, 64, LANES), f32),
            vmem((2, 3, LANES), f32),
            vmem((2, 3, LANES), f32),
            vmem((2, 16, LANES), f32),
            vmem((2, 3, 16, LANES), f32),
            vmem((2, 1, LANES), f32),
            vmem((2, 1, LANES), f32),
            vmem((2, 2, 1, LANES), f32),
            vmem((32, LANES), jnp.int32),
            vmem((32, LANES), f32),
            vmem((16, LANES), jnp.int32),
            vmem((16, LANES), f32),
            vmem((48, 32 * LANES), bf16),
            vmem((LANES, 32 * LANES), bf16),
            vmem((16, 16 * LANES), bf16),
            vmem((LANES, 16 * LANES), bf16),
            vmem((48, 16 * LANES), bf16),
            vmem((LANES, 16 * LANES), bf16),
            vmem((16, 16 * LANES), bf16),
            vmem((LANES, 16 * LANES), bf16),
            vmem((2, 48, 16 * LANES), bf16),
            vmem((2, LANES, 16 * LANES), bf16),
        ],
        compiler_params=pltpu.CompilerParams(collective_id=0, has_side_effects=True),
        name="newmark_step",
    )(*operands)
    outs = pl.pallas_call(
        write_kernel,
        out_shape=tuple(jax.ShapeDtypeStruct(shape, f32) for shape in shapes),
        in_specs=[pl.BlockSpec(memory_space=vmem)] * 4,
        out_specs=[pl.BlockSpec(memory_space=pl.ANY)] * 4,
        scratch_shapes=[pltpu.SemaphoreType.DMA((4,))],
        name="write_results",
    )(*[pltpu.with_memory_space_constraint(x, vmem) for x in outs])
    return outs[0], outs[1], outs[2].reshape(512), outs[3].reshape(512)


def solution(mesh):
    cut = ("region", "dom")
    line, plane = P(cut), P(None, cut)
    in_specs = (
        (plane,) * 3
        + (line,)
        + (plane,) * 3
        + (line,) * 5
        + (plane,) * 2
        + (line,)
        + (plane,) * 4
        + (P(None, None, cut),)
    )
    n_region, n_dom = mesh.shape["region"], mesh.shape["dom"]
    return jax.shard_map(
        lambda *args: on_device(n_region, n_dom, *args),
        mesh=mesh,
        in_specs=in_specs,
        out_specs=(plane, plane, line, line),
        check_vma=False,
    )
```

```python
import math

import jax
import jax.numpy as jnp
import numpy as np
from jax import lax
from jax.experimental import pallas as pl
from jax.experimental.pallas import tpu as pltpu
from jax.sharding import PartitionSpec as P

time_step = 0.4
MESH = pl.DeviceIdType.MESH
LANES = 128
f32 = jnp.float32
bf16 = jnp.bfloat16


def gll_tables():
    points = np.array([-1.0, -math.sqrt(3.0 / 7.0), 0.0, math.sqrt(3.0 / 7.0), 1.0])
    weights = np.array([0.1, 49.0 / 90.0, 32.0 / 45.0, 49.0 / 90.0, 0.1])
    products = np.array(
        [np.prod([points[i] - points[j] for j in range(5) if j != i]) for i in range(5)]
    )
    derivative = np.zeros((5, 5))
    for i in range(5):
        for j in range(5):
            if i != j:
                derivative[i, j] = products[i] / (products[j] * (points[i] - points[j]))
            else:
                derivative[i, j] = sum(1.0 / (points[i] - points[k]) for k in range(5) if k != i)
    weight_cube = weights[:, None, None] * weights[None, :, None] * weights[None, None, :]
    return derivative.astype(np.float32), weight_cube.astype(np.float32)


def derivative_matrices():
    derivative, weight_cube = gll_tables()
    eye = np.eye(5, dtype=np.float32)
    whole = np.zeros((3, LANES, LANES), np.float32)
    whole[0, :125, :125] = np.kron(derivative, np.kron(eye, eye))
    whole[1, :125, :125] = np.kron(eye, np.kron(derivative, eye))
    whole[2, :125, :125] = np.kron(eye, np.kron(eye, derivative))
    whole = whole.reshape(3 * LANES, LANES)
    high = whole.astype(jnp.bfloat16)
    low = (whole - high.astype(np.float32)).astype(jnp.bfloat16)
    weights = np.zeros((8, LANES), np.float32)
    weights[:, :125] = weight_cube.reshape(1, 125)
    return high, low, weights


def when(condition, action):
    if condition is None:
        action()
    else:
        pl.when(condition)(action)


def split(x):
    high = x.astype(bf16)
    return high, (x - high.astype(f32)).astype(bf16)


def dot(a, b, dims):
    return lax.dot_general(a, b, (dims, ((), ())), preferred_element_type=f32)


def dot_split(x, high, low, dims):
    x_high, x_low = split(x)
    return dot(x_high, high, dims) + dot(x_low, high, dims) + dot(x_high, low, dims)


def lookup(tables, hi, lo):
    out = [jnp.zeros(hi.shape, f32) for _ in tables]
    for h in range(len(tables[0])):
        here = hi == h
        for c, rows in enumerate(tables):
            picked = jnp.take_along_axis(
                jnp.broadcast_to(rows[h], hi.shape), lo, axis=1, mode="promise_in_bounds"
            )
            out[c] = jnp.where(here, picked, out[c])
    return out


def mark_low(marks_ref, lo):
    shape = (marks_ref.shape[0], LANES)
    sublane = lax.broadcasted_iota(jnp.int32, shape, 0)
    for row in range(lo.shape[0]):
        line = jnp.broadcast_to(lo[row : row + 1], shape)
        marks_ref[:, row * LANES : (row + 1) * LANES] = jnp.where(line == sublane, 1.0, 0.0).astype(
            bf16
        )


def spread_high(terms_ref, hi, values):
    sublane = lax.broadcasted_iota(jnp.int32, (8, LANES), 0)
    parts = []
    for value in values:
        high = value.astype(bf16).astype(f32)
        parts.append((high, value - high))
    for row in range(hi.shape[0]):
        here = jnp.broadcast_to(hi[row : row + 1], (8, LANES)) == sublane
        for c, pair in enumerate(parts):
            both = [
                jnp.where(here, jnp.broadcast_to(part[row : row + 1], (8, LANES)), 0.0)
                for part in pair
            ]
            terms_ref[16 * c : 16 * c + 16, row * LANES : (row + 1) * LANES] = jnp.concatenate(
                both, axis=0
            ).astype(bf16)


def halved(terms_ref, marks_ref):
    middle = terms_ref.shape[1] // 2
    return sum(
        dot(terms_ref[:, half], marks_ref[:, half], ((1,), (1,)))
        for half in (slice(0, middle), slice(middle, 2 * middle))
    )


def collect(terms_ref, marks_ref):
    sums = halved(terms_ref, marks_ref)
    return [
        sums[16 * c : 16 * c + 8] + sums[16 * c + 8 : 16 * c + 16]
        for c in range(terms_ref.shape[0] // 16)
    ]


def spread_rows(terms_ref, values):
    sublane = lax.broadcasted_iota(jnp.int32, (8, LANES), 0)
    for c, value in enumerate(values):
        high = value.astype(bf16).astype(f32)
        pair = (high, value - high)
        for row in range(value.shape[0]):
            first = row // 8 * 8
            both = [
                jnp.where(sublane == row % 8, part[first : first + 8], 0.0) for part in pair
            ]
            terms_ref[16 * c : 16 * c + 16, row * LANES : (row + 1) * LANES] = jnp.concatenate(
                both, axis=0
            ).astype(bf16)


def rows_of(ref, lead):
    line = ref[lead]
    return jnp.concatenate([line[:, LANES * t : LANES * (t + 1)] for t in range(8)], axis=0)


def both_sides(ref, *lead):
    return jnp.concatenate(
        [rows_of(ref, (*lead, slice(p, p + 1), slice(None))) for p in range(2)], axis=0
    )


def step_kernel(n_region, n_dom, n_inputs, local, *refs):
    load_sem, send_sem = local
    sources = refs[:n_inputs]
    velocity_out, acceleration_out, dot_out, ddot_out = refs[n_inputs : n_inputs + 4]
    held = refs[n_inputs + 4 : 2 * n_inputs + 4]
    (
        passed_sem,
        known_sem,
        recv_sem,
        motion_send,
        motion_recv,
        static_send,
        static_recv,
        normals_send,
        normals_recv,
        rims_send,
        rims_recv,
        block_send,
        block_recv,
        fluid_send,
        fluid_recv,
        far_recv,
        index_pad,
        field_pad,
        fluid_index_pad,
        fluid_field_pad,
        element_terms,
        element_marks,
        fluid_terms,
        fluid_marks,
        slot_terms,
        slot_marks,
        arrived_terms,
        arrived_marks,
        near_terms,
        near_marks,
    ) = refs[2 * n_inputs + 4 :]
    (
        displacement,
        velocity,
        acceleration,
        solid_interface,
        interface_normal,
        potential,
        potential_dot,
        potential_ddot,
        fluid_connectivity,
        density_inverse,
        fluid_inverse_size,
        matrix_high,
        matrix_low,
        weight_cube,
        fluid_interface,
        fluid_halo,
        fluid_mass_inverse,
        connectivity,
        lame_lambda,
        shear_modulus,
        inverse_size,
        solid_halo,
        solid_mass_inverse,
    ) = held

    region, dom = lax.axis_index("region"), lax.axis_index("dom")
    has_above, has_below = region < n_region - 1, region > 0
    to_region = {1: (has_above, has_below), -1: (has_below, has_above), 0: (None, None)}
    device = {
        (up, along): (
            region + up,
            lax.rem(dom + n_dom + along, n_dom),
        )
        for up in (-1, 0, 1)
        for along in (-2, -1, 0, 1, 2)
    }
    for ref in (motion_recv, static_recv, block_recv, far_recv):
        ref[...] = jnp.zeros(ref.shape, f32)
    barrier = pltpu.get_barrier_semaphore()
    for (up, along), other in device.items():
        if abs(up) + abs(along) == 1:
            when(
                to_region[up][0],
                lambda other=other: pl.semaphore_signal(
                    barrier, inc=1, device_id=other, device_id_type=MESH
                ),
            )
    loads = [
        pltpu.make_async_copy(source, target, load_sem.at[i])
        for i, (source, target) in enumerate(zip(sources, held))
    ]
    for load in loads:
        load.start()

    started = []

    def send(*messages):
        copies = []
        for source, target, up, along in messages:
            number = len(started)
            copy = pltpu.make_async_remote_copy(
                src_ref=source,
                dst_ref=target,
                send_sem=send_sem.at[number],
                recv_sem=recv_sem.at[number],
                device_id=device[up, along],
                device_id_type=MESH,
            )
            when(to_region[up][0], copy.start)
            started.append((copy, to_region[up][0]))
            copies.append((copy, to_region[up][1]))
        return copies

    def receive(copies):
        for copy, condition in copies:
            when(condition, copy.wait_recv)

    for i in range(5):
        loads[i].wait()
    half_square = 0.5 * time_step * time_step
    predicted = displacement[...] + time_step * velocity[...] + half_square * acceleration[...]
    solid_tables = [
        [predicted[c : c + 1, LANES * h : LANES * (h + 1)] for h in range(8)] for c in range(3)
    ]
    slots = both_sides(solid_interface)
    slot_hi, slot_lo = slots >> 7, slots & 127
    normals = [both_sides(interface_normal, c) for c in range(3)]
    moved = lookup(solid_tables, slot_hi, slot_lo)
    motion = normals[0] * moved[0] + normals[1] * moved[1] + normals[2] * moved[2]
    motion_send[0] = motion[8:]
    motion_send[1] = motion[:8]

    peers = 2 + lax.div(region + n_region - 1, n_region)
    peers = peers + lax.div(2 * n_region - 2 - region, n_region)
    pl.semaphore_wait(barrier, peers)

    def greet(semaphore):
        for along in (-1, 1):
            pl.semaphore_signal(
                semaphore, inc=1, device_id=device[0, along], device_id_type=MESH
            )

    greet(passed_sem)
    motion_copies = send(
        (motion_send.at[0], motion_recv.at[0], 1, 0),
        (motion_send.at[1], motion_recv.at[1], -1, 0),
    )

    for i in range(5, 14):
        loads[i].wait()
    fluid_predicted = (
        potential[...] + time_step * potential_dot[...] + half_square * potential_ddot[...]
    )
    fluid_table = [[fluid_predicted[h : h + 1] for h in range(4)]]
    fluid_index_pad[...] = jnp.full(fluid_index_pad.shape, -1, jnp.int32)
    fluid_index_pad[:, :125] = fluid_connectivity[...]
    fluid_field_pad[...] = jnp.zeros(fluid_field_pad.shape, f32)
    fluid_field_pad[:, :125] = density_inverse[...].astype(f32)
    fluid_index = fluid_index_pad[...]
    fluid_hi, fluid_lo = fluid_index >> 7, fluid_index & 127
    local = lookup(fluid_table, fluid_hi, fluid_lo)[0]
    high, low = matrix_high[...], matrix_low[...]
    gradient = dot_split(local, high, low, ((1,), (1,)))

    def column(line, count):
        rows = lax.broadcasted_iota(jnp.int32, (count, count), 0)
        columns = lax.broadcasted_iota(jnp.int32, (count, count), 1)
        wide = jnp.broadcast_to(line, (count, count))
        return jnp.sum(jnp.where(rows == columns, wide, 0.0), axis=1, keepdims=True)

    weights = weight_cube[0:1]
    fluid_factor = weights * fluid_field_pad[...] * (-1.0 / column(fluid_inverse_size[...], 16))
    weighted = jnp.concatenate(
        [gradient[:, LANES * b : LANES * (b + 1)] * fluid_factor for b in range(3)], axis=1
    )
    element = dot_split(weighted, high, low, ((1,), (0,)))
    mark_low(fluid_marks, fluid_lo)
    spread_high(fluid_terms, fluid_hi, [element])
    fluid_force = collect(fluid_terms, fluid_marks)[0]

    def rim_index(halo_ref, pad_ref, count):
        pad_ref[...] = jnp.full(pad_ref.shape, -1, jnp.int32)
        pad_ref[0:2, :count] = halo_ref[...]
        return pad_ref[...]

    def slot_of_node(rim):
        out = []
        marks_lane = lax.broadcasted_iota(jnp.int32, (LANES, LANES), 0)
        sublane = lax.broadcasted_iota(jnp.int32, (8, LANES), 0)
        number = lax.broadcasted_iota(jnp.int32, (8, LANES), 1).astype(f32) + 1.0
        for side in range(2):
            line = rim[side : side + 1]
            marks = jnp.where(
                jnp.broadcast_to(line & 127, (LANES, LANES)) == marks_lane, 1.0, 0.0
            ).astype(bf16)
            terms = jnp.where(jnp.broadcast_to(line >> 7, (8, LANES)) == sublane, number, 0.0)
            out.append(dot(terms.astype(bf16), marks, ((1,), (1,))))
        return out

    def pick(line, place):
        index = jnp.maximum(place.astype(jnp.int32) - 1, 0)
        wide = jnp.broadcast_to(line, place.shape)
        picked = jnp.take_along_axis(wide, index, axis=1, mode="promise_in_bounds")
        return jnp.where(place > 0.5, picked, 0.0)

    for i in range(14, 17):
        loads[i].wait()
    fluid_slots = both_sides(fluid_interface)
    arrived_hi, arrived_lo = fluid_slots >> 7, fluid_slots & 127
    fluid_rim = rim_index(fluid_halo, index_pad.at[0:8], 48)
    fluid_places = slot_of_node(fluid_rim)
    slot_mass = lookup(
        [[fluid_mass_inverse[h : h + 1] for h in range(4)]]
        + [[place[h : h + 1] for h in range(4)] for place in fluid_places],
        arrived_hi,
        arrived_lo,
    )
    for i in range(3):
        static_send[0, 8 * i : 8 * i + 8] = slot_mass[i][8:]
        static_send[1, 8 * i : 8 * i + 8] = slot_mass[i][:8]
    loads[21].wait()
    solid_rim = rim_index(solid_halo, index_pad.at[0:8], 96)
    solid_places = slot_of_node(solid_rim)
    slot_places = lookup(
        [[place[h : h + 1] for h in range(8)] for place in solid_places], slot_hi, slot_lo
    )
    for side in range(2):
        for c in range(3):
            normals_send[side, 16 * c : 16 * c + 16] = -normals[c]
        normals_send[side, 48:] = slot_places[1 - side]

    pl.semaphore_wait(passed_sem, 2)
    greet(known_sem)
    normals_copies = send(
        *((normals_send.at[i], normals_recv.at[i], 0, 1 - 2 * i) for i in range(2))
    )
    static_copies = send(
        *(
            (static_send.at[i], static_recv.at[i, 1 + along], 1 - 2 * i, along)
            for along in (-1, 0, 1)
            for i in range(2)
        )
    )

    for i in (17, 18, 19, 20, 22):
        loads[i].wait()
    index_pad[...] = jnp.full(index_pad.shape, -1, jnp.int32)
    index_pad[:, :125] = connectivity[...]
    index = index_pad[...]
    hi, lo = index >> 7, index & 127
    values = lookup(solid_tables, hi, lo)
    gradient = dot_split(jnp.concatenate(values, axis=0), high, low, ((1,), (1,)))
    field_pad[...] = jnp.zeros(field_pad.shape, f32)
    field_pad[:, :125] = lame_lambda[...].astype(f32)
    lame = field_pad[...]
    field_pad[:, :125] = shear_modulus[...].astype(f32)
    shear = field_pad[...]
    factor = weights * (-1.0 / column(inverse_size[...], 32))
    lame, shear = lame * factor, shear * factor
    grad = [
        [gradient[32 * c : 32 * c + 32, LANES * b : LANES * (b + 1)] for b in range(3)]
        for c in range(3)
    ]
    trace = lame * (grad[0][0] + grad[1][1] + grad[2][2])
    stress = [[None] * 3 for _ in range(3)]
    for a in range(3):
        stress[a][a] = trace + shear * (grad[a][a] + grad[a][a])
        for b in range(a):
            stress[a][b] = stress[b][a] = shear * (grad[a][b] + grad[b][a])
    weighted = jnp.concatenate([jnp.concatenate(row, axis=1) for row in stress], axis=0)
    element = dot_split(weighted, high, low, ((1,), (0,)))
    mark_low(element_marks, lo)
    spread_high(element_terms, hi, [element[32 * c : 32 * c + 32] for c in range(3)])

    force = collect(element_terms, element_marks)
    rim_values = lookup(
        [[t[h : h + 1] for h in range(8)] for t in force], solid_rim >> 7, solid_rim & 127
    )
    for c in range(3):
        rims_send[0, c : c + 1] = rim_values[c][1:2]
        rims_send[1, c : c + 1] = rim_values[c][0:1]
    rims_copies = send(*((rims_send.at[i], rims_recv.at[i], 0, 1 - 2 * i) for i in range(2)))
    mark_low(arrived_marks, arrived_lo)

    pl.semaphore_wait(known_sem, 2)
    receive(motion_copies)
    spread_high(
        arrived_terms, arrived_hi, [jnp.concatenate([motion_recv[0], motion_recv[1]], axis=0)]
    )
    fluid_total = fluid_force + collect(arrived_terms, arrived_marks)[0]
    total_rows = [[fluid_total[h : h + 1] for h in range(4)]]
    at_slots = lookup(total_rows, arrived_hi, arrived_lo)[0]
    rim_values = lookup(total_rows, fluid_rim >> 7, fluid_rim & 127)[0]
    for i in range(2):
        block_send[i, :8] = at_slots[8 - 8 * i : 16 - 8 * i]
        block_send[i, 8:9] = rim_values[1:2]
        block_send[i, 9:10] = rim_values[0:1]
        fluid_send[i] = rim_values[1 - i : 2 - i]
    block_copies = send(
        *(
            (fluid_send.at[j], far_recv.at[i, j], 1 - 2 * i, 2 - 4 * j)
            for j in range(2)
            for i in range(2)
        ),
        *(
            (block_send.at[i], block_recv.at[i, 1 + along], 1 - 2 * i, along)
            for along in (-1, 1, 0)
            for i in range(2)
        ),
    )
    fluid_copies = send(*((fluid_send.at[i], fluid_recv.at[i], 0, 1 - 2 * i) for i in range(2)))

    mark_low(slot_marks, slot_lo)
    receive(normals_copies)
    for i in range(2):
        mark_low(near_marks.at[i], normals_recv[i, 48:].astype(jnp.int32) - 1)
    mass = solid_mass_inverse[...]
    base = [
        rows_of(velocity, (slice(c, c + 1), slice(None)))
        + 0.5 * time_step * rows_of(acceleration, (slice(c, c + 1), slice(None)))
        for c in range(3)
    ]
    receive(fluid_copies)
    assembled = fluid_total
    for i in range(2):
        assembled = assembled + pick(fluid_recv[i], fluid_places[i])
    ddot = fluid_mass_inverse[...] * assembled[:4]
    ddot_out[...] = ddot
    dot_out[...] = potential_dot[...] + 0.5 * time_step * (potential_ddot[...] + ddot)
    receive(static_copies)
    receive(rims_copies)

    receive(block_copies)

    def pressure_of(column):
        sides = []
        for i in range(2):
            block = block_recv.at[i, 1 - column]
            if column == -1:
                low_rim = far_recv[i, 0]
            else:
                low_rim = block_recv[i, 2 - column, 8:9]
            if column == 1:
                high_rim = far_recv[i, 1]
            else:
                high_rim = block_recv[i, -column, 9:10]
            slot_mass, low_place, high_place = (
                static_recv[i, 1 - column, 8 * j : 8 * j + 8] for j in range(3)
            )
            value = block[:8] + pick(low_rim, low_place)
            sides.append(slot_mass * (value + pick(high_rim, high_place)))
        return jnp.concatenate(sides, axis=0)

    arrived = pressure_of(0)
    spread_high(slot_terms, slot_hi, [-(normal * arrived) for normal in normals])
    for i in range(2):
        arrived = pressure_of(2 * i - 1)
        spread_rows(
            near_terms.at[i],
            [normals_recv[i, 16 * c : 16 * c + 16] * arrived for c in range(3)],
        )
    blank = jnp.zeros((1, LANES - 96), f32)
    near = []
    for i in range(2):
        sums = dot(near_terms[i], near_marks[i], ((1,), (1,)))
        near.append(
            [jnp.sum(sums[16 * c : 16 * c + 16], axis=0, keepdims=True) for c in range(3)]
        )
    coupling = collect(slot_terms, slot_marks)
    for c in range(3):
        assembled = force[c] + coupling[c]
        for i in range(2):
            line = rims_recv[i, c : c + 1] + jnp.concatenate([near[i][c], blank], axis=1)
            assembled = assembled + pick(line, solid_places[i])
        new = mass * assembled
        speed = base[c] + 0.5 * time_step * new
        for h in range(8):
            acceleration_out[c : c + 1, LANES * h : LANES * (h + 1)] = new[h : h + 1]
            velocity_out[c : c + 1, LANES * h : LANES * (h + 1)] = speed[h : h + 1]
    for copy, condition in started:
        when(condition, copy.wait_send)


def write_kernel(*refs):
    sem = refs[-1]
    copies = [
        pltpu.make_async_copy(refs[i], refs[4 + i], sem.at[i]) for i in range(4)
    ]
    for copy in copies:
        copy.start()
    for copy in copies:
        copy.wait()


def on_device(
    n_region,
    n_dom,
    displacement,
    velocity,
    acceleration,
    solid_mass_inverse,
    connectivity,
    lame_lambda,
    shear_modulus,
    inverse_size,
    potential,
    potential_dot,
    potential_ddot,
    fluid_mass_inverse,
    fluid_connectivity,
    density_inverse,
    fluid_inverse_size,
    solid_halo,
    fluid_halo,
    solid_interface,
    fluid_interface,
    interface_normal,
):
    high, low, weights = derivative_matrices()
    operands = (
        displacement,
        velocity,
        acceleration,
        solid_interface,
        interface_normal,
        potential.reshape(4, LANES),
        potential_dot.reshape(4, LANES),
        potential_ddot.reshape(4, LANES),
        fluid_connectivity.T,
        density_inverse.T,
        fluid_inverse_size.reshape(1, 16),
        jnp.asarray(high),
        jnp.asarray(low),
        jnp.asarray(weights),
        fluid_interface,
        fluid_halo,
        fluid_mass_inverse.reshape(4, LANES),
        connectivity.T,
        lame_lambda.T,
        shear_modulus.T,
        inverse_size.reshape(1, 32),
        solid_halo,
        solid_mass_inverse.reshape(8, LANES),
    )
    count = len(operands)
    vmem = pltpu.VMEM
    shapes = ((3, 1024), (3, 1024), (4, LANES), (4, LANES))
    outs = pl.pallas_call(
        lambda *refs: pl.run_scoped(
            lambda *local: step_kernel(n_region, n_dom, count, local, *refs),
            pltpu.SemaphoreType.DMA((count,)),
            pltpu.SemaphoreType.DMA((24,)),
        ),
        out_shape=tuple(pltpu.VMEM(shape, f32) for shape in shapes),
        in_specs=[pl.BlockSpec(memory_space=pl.ANY)] * count,
        out_specs=[pl.BlockSpec(memory_space=vmem)] * 4,
        scratch_shapes=[vmem(x.shape, x.dtype) for x in operands]
        + [
            pltpu.SemaphoreType.REGULAR,
            pltpu.SemaphoreType.REGULAR,
            pltpu.SemaphoreType.DMA((24,)),
            vmem((2, 8, LANES), f32),
            vmem((2, 8, LANES), f32),
            vmem((2, 24, LANES), f32),
            vmem((2, 3, 24, LANES), f32),
            vmem((2, 64, LANES), f32),
            vmem((2, 64, LANES), f32),
            vmem((2, 3, LANES), f32),
            vmem((2, 3, LANES), f32),
            vmem((2, 16, LANES), f32),
            vmem((2, 3, 16, LANES), f32),
            vmem((2, 1, LANES), f32),
            vmem((2, 1, LANES), f32),
            vmem((2, 2, 1, LANES), f32),
            vmem((32, LANES), jnp.int32),
            vmem((32, LANES), f32),
            vmem((16, LANES), jnp.int32),
            vmem((16, LANES), f32),
            vmem((48, 32 * LANES), bf16),
            vmem((LANES, 32 * LANES), bf16),
            vmem((16, 16 * LANES), bf16),
            vmem((LANES, 16 * LANES), bf16),
            vmem((48, 16 * LANES), bf16),
            vmem((LANES, 16 * LANES), bf16),
            vmem((16, 16 * LANES), bf16),
            vmem((LANES, 16 * LANES), bf16),
            vmem((2, 48, 16 * LANES), bf16),
            vmem((2, 96, 16 * LANES), bf16),
        ],
        compiler_params=pltpu.CompilerParams(collective_id=0, has_side_effects=True),
        name="newmark_step",
    )(*operands)
    outs = pl.pallas_call(
        write_kernel,
        out_shape=tuple(jax.ShapeDtypeStruct(shape, f32) for shape in shapes),
        in_specs=[pl.BlockSpec(memory_space=vmem)] * 4,
        out_specs=[pl.BlockSpec(memory_space=pl.ANY)] * 4,
        scratch_shapes=[pltpu.SemaphoreType.DMA((4,))],
        name="write_results",
    )(*[pltpu.with_memory_space_constraint(x, vmem) for x in outs])
    return outs[0], outs[1], outs[2].reshape(512), outs[3].reshape(512)


def solution(mesh):
    cut = ("region", "dom")
    line, plane = P(cut), P(None, cut)
    in_specs = (
        (plane,) * 3
        + (line,)
        + (plane,) * 3
        + (line,) * 5
        + (plane,) * 2
        + (line,)
        + (plane,) * 4
        + (P(None, None, cut),)
    )
    n_region, n_dom = mesh.shape["region"], mesh.shape["dom"]
    return jax.shard_map(
        lambda *args: on_device(n_region, n_dom, *args),
        mesh=mesh,
        in_specs=in_specs,
        out_specs=(plane, plane, line, line),
        check_vma=False,
    )
```
